32 devices in a mesh: ctx: 16 (over z, y, x), dp: 2 (over core).
Axes of the slice: x: 2, y: 2, z: 4, core: 2. Of those that a mesh axis runs over, the one named last changes fastest.
Arguments:
- signal: bfloat16 [2, 2048, 4096], P('dp', 'ctx'), may hold values from -6 to 6
- cotangent: bfloat16 [2, 2048, 4096], P('dp', 'ctx'), may hold values from -6 to 6
- record_id: int32 [2, 2048], P('dp', 'ctx'), may hold values from 0 to 3, never falling along the last dimension, each value on 1 to 1024 neighbouring positions
- rate: float32 [32, 16], replicated, may hold values from 9.765625e-05 to 0.046875, as said below
- residue: float32 [32, 16], replicated, may hold values from -1 to 1
Outputs:
- signal_grad: bfloat16 [2, 2048, 4096], P('dp', 'ctx')
- residue_grad: float32 [32, 16], replicated
The draws below stay inside these ranges and needn't reach their ends.
Inputs may be any that keep to these rules, and one draw needn't show every extreme that they name: `record_id`: along each sequence the ids never fall; each record covers 1 to 1024 consecutive positions, and one covers exactly 1024. `rate`: positive rates.
All inputs are finite; a program needn't handle non-finite values.
Results may differ from the reference program's by a relative error of at most 0.008.
Values sent between devices are 32-bit elements; how exact they have to be, the bound alone decides.
A program may use at most 192 MiB of HBM per device.

```python
import math
import jax
import jax.numpy as jnp
import numpy as np
from jax import lax

DW = 4096
GW = 128
ORDER = 16
TOK_DEV = 128
FILTERS = 32
BATCH = 2
SEQ_LEN = 2048
REC_MAX = 1024
RECORDS = 4
TOKENS = 4096


def draw_rate(key, part):
    key_pick = jax.random.fold_in(key, 11)
    key_level = jax.random.fold_in(key, 23)
    fast_share = 0.5
    picker = jax.random.uniform(key_pick, (FILTERS, ORDER), jnp.float32)
    level = jax.random.uniform(key_level, (FILTERS, ORDER), jnp.float32)
    slow_rate = jnp.exp(jnp.log(0.1 / REC_MAX) + level * jnp.log(20.0))
    fast_rate = jnp.exp(jnp.log(3.0 / TOK_DEV) + level * jnp.log(2.0))
    return jnp.where(picker < fast_share, fast_rate, slow_rate).astype(jnp.float32)


def block_scale(stream_key, shape, shards, least, top_value):
    gain = 1.0
    for dim, shards_of in shards:
        steps = jax.random.uniform(jax.random.fold_in(jax.random.fold_in(stream_key, 6), dim), (shards_of,), jnp.float32, least / len(shards), top_value / len(shards))
        gain = gain * jnp.repeat(jnp.exp(steps), shape[dim] // shards_of).reshape((-1,) + (1,) * (len(shape) - 1 - dim))
    return gain


def split_up(number_of, total, reach, slope):
    loads = [(1 << 20) // math.isqrt(grade ** slope) + 1 for grade in range(2, number_of + 1)]
    surplus, counts = total - reach - (number_of - 1), [1] * (number_of - 1)
    while surplus > 0:
        candidates = [i for i in range(number_of - 1) if counts[i] < reach]
        mass, remaining = sum([loads[i] for i in candidates]), surplus
        for i in candidates:
            addition = min(reach - counts[i], max(1, remaining * loads[i] // mass), surplus)
            counts[i] = counts[i] + addition
            surplus = surplus - addition
    return np.array([reach] + counts)


def uneven(key, count, total, most, slope):
    if count == 2:
        one = jax.random.randint(key, (), max(1, total - most), min(most, total - 1) + 1)
        return jnp.stack([one, total - one])
    sizes = jnp.asarray(split_up(count, total, most, slope), jnp.int32)
    twos = (count - 1) // 2
    source_of, taker = sizes[1:1 + 2 * twos:2], sizes[2:2 + 2 * twos:2]
    margin = jnp.minimum(source_of - 1, most - taker)
    moved = jax.random.randint(jax.random.fold_in(key, 1), (twos,), 0, 1 << 20) % (margin + 1)
    sizes = sizes.at[1:1 + 2 * twos:2].set(source_of - moved).at[2:2 + 2 * twos:2].set(taker + moved)
    return sizes[jax.random.permutation(jax.random.fold_in(key, 2), count)]


def normal_values(rng, shape, width, bound, shards=(), kind=jnp.bfloat16):
    loudness = block_scale(rng, shape, shards, -0.22, 0.18) if shards else 1.0
    drawn = jax.random.normal(rng, shape, jnp.float32) * width * loudness
    return jnp.minimum(jnp.maximum(drawn, -bound), bound).astype(kind)


def setup_inputs(seed: int = 0) -> dict:
    streams_of = jax.random.split(jax.random.key(seed), 6)
    signal = normal_values(streams_of[0], (BATCH, SEQ_LEN, DW), 1.0, 6.0, ((0, 2), (1, 16)))
    cotangent = normal_values(streams_of[1], (BATCH, SEQ_LEN, DW), 1.0, 6.0, ((0, 2), (1, 16)))
    record_id = jax.vmap(lambda own: jnp.searchsorted(jnp.cumsum(uneven(own, RECORDS, SEQ_LEN, REC_MAX, 1)), jnp.arange(SEQ_LEN), side="right"))(jax.random.split(streams_of[2], BATCH)).reshape((BATCH, SEQ_LEN)).astype(jnp.int32)
    rate = draw_rate(jax.random.fold_in(streams_of[5], 71), 0)
    residue = normal_values(streams_of[4], (FILTERS, ORDER), 0.25, 1.0, (), jnp.float32)
    return {"signal": signal, "cotangent": cotangent, "record_id": record_id, "rate": rate, "residue": residue}


HIGH = lax.Precision.HIGHEST

def block_tables(block_records, rate, residue):
    length = block_records.shape[0]
    position = jnp.arange(length, dtype=jnp.float32)
    first_id = block_records[0]
    last_id = block_records[length - 1]
    in_first = (block_records == first_id).astype(jnp.float32)
    in_last = (block_records == last_id).astype(jnp.float32)
    lag_matrix = position[:, None] - position[None, :]
    linked = ((block_records[:, None] == block_records[None, :]) & (lag_matrix >= 0)).astype(jnp.float32)
    norm_coef = jnp.sqrt(-jnp.expm1(-2.0 * rate))
    weights = residue * norm_coef
    end_weight = jnp.exp(-rate[:, :, None] * (length - 1 - position)[None, None, :]) * in_last[None, None, :]
    start_weight = jnp.exp(-rate[:, :, None] * (position + 1.0)[None, None, :]) * in_first[None, None, :]
    through = jnp.exp(-rate * length) * (first_id == last_id).astype(jnp.float32)
    return (lag_matrix, linked, norm_coef, weights, end_weight, start_weight, through)

def reference(signal, cotangent, record_id, rate, residue):
    blocks = SEQ_LEN // TOK_DEV

    def one_sequence(inputs):
        tokens, grad_rows, records = inputs
        tokens_f = tokens.astype(jnp.float32).reshape(blocks, TOK_DEV, FILTERS, GW)
        grads_f = grad_rows.astype(jnp.float32).reshape(blocks, TOK_DEV, FILTERS, GW)
        block_ids = records.reshape(blocks, TOK_DEV)

        def forward_step(carry, inputs_now):
            state_now, prev_last = carry
            block_tokens, block_records = inputs_now
            tables = block_tables(block_records, rate, residue)
            end_weight, through = (tables[4], tables[6])
            carried = state_now * (prev_last == block_records[0]).astype(jnp.float32)
            end_state = jnp.einsum('gns,sgc->gnc', end_weight, block_tokens, precision=HIGH)
            return ((through[:, :, None] * carried + end_state, block_records[TOK_DEV - 1]), carried)
        start_carry = (jnp.zeros((FILTERS, ORDER, GW), jnp.float32), jnp.int32(-1))
        unused_one, carried_all = lax.scan(forward_step, start_carry, (tokens_f, block_ids))

        def backward_step(carry, inputs_now):
            pending, next_first = carry
            block_grads, block_records = inputs_now
            tables = block_tables(block_records, rate, residue)
            weights, start_weight, through = (tables[3], tables[5], tables[6])
            adjoint = pending * (next_first == block_records[TOK_DEV - 1]).astype(jnp.float32)
            start_sens = jnp.einsum('gnt,tgc->gnc', start_weight, block_grads, precision=HIGH)
            new_pending = weights[:, :, None] * start_sens + through[:, :, None] * adjoint
            return ((new_pending, block_records[0]), adjoint)
        unused_two, adjoint_all = lax.scan(backward_step, start_carry, (grads_f, block_ids), reverse=True)

        def block_output(inputs_now):
            block_tokens, block_grads, block_records, carried, adjoint = inputs_now
            lag_matrix, linked, norm_coef, weights, end_weight, start_weight, through = block_tables(block_records, rate, residue)
            decay_full = jnp.exp(-rate[:, :, None, None] * jnp.maximum(lag_matrix, 0.0)[None, None]) * linked[None, None]
            kernel = jnp.einsum('gn,gnts->gts', weights, decay_full, precision=HIGH)
            local = jnp.einsum('gts,tgc->sgc', kernel, block_grads, precision=HIGH)
            local = local + jnp.einsum('gns,gnc->sgc', end_weight, adjoint, precision=HIGH)
            products = jnp.einsum('tgc,sgc->gts', block_grads, block_tokens, precision=HIGH)
            intra_term = jnp.einsum('gts,gnts->gn', products, decay_full, precision=HIGH)
            start_sens = jnp.einsum('gnt,tgc->gnc', start_weight, block_grads, precision=HIGH)
            carry_term = lax.optimization_barrier(jnp.sum(start_sens * carried, axis=2))
            return (local.reshape(TOK_DEV, DW).astype(jnp.bfloat16), norm_coef * (intra_term + carry_term))
        grad_blocks, block_terms = lax.map(block_output, (tokens_f, grads_f, block_ids, carried_all, adjoint_all))
        return (grad_blocks.reshape(SEQ_LEN, DW), lax.optimization_barrier(jnp.sum(block_terms, axis=0)))
    signal_grad, seq_terms = lax.map(one_sequence, (signal, cotangent, record_id))
    residue_grad = lax.optimization_barrier(jnp.sum(seq_terms, axis=0)) / jnp.sqrt(jnp.float32(TOKENS * GW))
    return (signal_grad, residue_grad)
```

```python
import functools
import math

import jax
import jax.numpy as jnp
from jax import lax
from jax.experimental import pallas as pl
from jax.experimental.pallas import tpu as pltpu
from jax.sharding import PartitionSpec as P

CLUSTER = 4
PIECES = 4
MESH = pl.DeviceIdType.MESH
F32 = jnp.float32
BF16 = jnp.bfloat16


def two_parts(table):
    high = table.astype(BF16)
    return high, (table - high.astype(F32)).astype(BF16)


def dot(left, right, contract=((1,), (0,))):
    return lax.dot_general(left, right, (contract, ((), ())), preferred_element_type=F32)


def kernel(
    filters,
    modes,
    shards,
    scale,
    copies,
    signal_hbm,
    cotangent_hbm,
    record_hbm,
    rate_hbm,
    residue_hbm,
    grad_ref,
    term_ref,
    signal_ref,
    cotangent_ref,
    record_ref,
    rate_ref,
    residue_ref,
    rates,
    weights,
    mask,
    flip,
    flipped_mask,
    local,
    ends,
    intra,
    sens_out,
    sens_in,
    sum_out,
    sum_in,
    adj_out,
    adj_in,
    sens_send,
    sens_recv,
    sum_send,
    sum_recv,
    adj_send,
    adj_recv,
    near_out,
    near_in,
    far_in,
    near_send,
    near_recv,
    far_send,
    far_recv,
    fetch_sem,
):
    fetches = [
        pltpu.make_async_copy(source, target, fetch_sem.at[place])
        for place, (source, target) in enumerate(
            (
                (record_hbm, record_ref),
                (rate_hbm, rate_ref),
                (residue_hbm, residue_ref),
                (cotangent_hbm, cotangent_ref),
                (signal_hbm, signal_ref),
            )
        )
    ]
    for fetch in fetches:
        fetch.start()
    length = signal_ref.shape[0]
    width = signal_ref.shape[1] // filters
    share = filters // CLUSTER
    rows = share * modes
    me = lax.axis_index("ctx")
    mine = lax.rem(me, CLUSTER)
    home = me - mine
    clusters = shards // CLUSTER
    block = me // CLUSTER
    copy_of = lax.axis_index("dp")
    near_count = CLUSTER * copies
    near_mine = copy_of * CLUSTER + mine

    def near_spot(step):
        rank = lax.rem(near_mine + step, near_count)
        return {"ctx": home + lax.rem(rank, CLUSTER), "dp": rank // CLUSTER}

    def far_spot(step):
        return {"ctx": lax.rem(block + step, clusters) * CLUSTER + mine, "dp": copy_of}

    barrier = pltpu.get_barrier_semaphore()
    for step in range(1, near_count):
        pl.semaphore_signal(barrier, inc=1, device_id=near_spot(step), device_id_type=MESH)
    for step in range(1, clusters):
        pl.semaphore_signal(barrier, inc=1, device_id=far_spot(step), device_id_type=MESH)

    lane = lax.broadcasted_iota(jnp.int32, (modes, length), 1).astype(F32)
    filter_lane = lax.broadcasted_iota(jnp.int32, (modes, filters), 1)
    for fetch in fetches[:3]:
        fetch.wait()
    ids = jnp.broadcast_to(record_ref[...].astype(F32), (length, length))
    first = ids[:8, :1]
    last = ids[:8, length - 1 :]
    in_first = (ids[:1] == first[:1]).astype(F32)
    in_last = (ids[:1] == last[:1]).astype(F32)
    row = lax.broadcasted_iota(jnp.int32, (length, length), 0)
    column = lax.broadcasted_iota(jnp.int32, (length, length), 1)
    mask[...] = jnp.where((ids == ids.T) & (column >= row), 1.0, 0.0)
    flip[...] = jnp.where(row + column == length - 1, 1.0, 0.0).astype(BF16)
    flipped_mask[...] = dot(flip[...], mask[...].astype(BF16))
    tag_row = lax.broadcasted_iota(jnp.int32, (8, width), 0)
    tag = jnp.where(tag_row == 0, first, last)

    def group(index):
        return pl.ds(pl.multiple_of(index * width, width), width)

    def table_rows(index):
        return pl.ds(pl.multiple_of(index * modes, modes), modes)

    def column_of(ref, index):
        return jnp.sum(jnp.where(filter_lane == index, ref[...], 0.0), axis=1, keepdims=True)

    def norm_of(rate):
        double = 2.0 * rate
        series = 1.0 - double * (1.0 / 6.0) * (1.0 - double * (1.0 / 7.0))
        for divisor in (5.0, 4.0, 3.0, 2.0):
            series = 1.0 - double * (1.0 / divisor) * series
        return jnp.sqrt(double * series)

    def sense(index, carry):
        rate = jnp.broadcast_to(column_of(rate_ref, index), (modes, width))
        rates[table_rows(index), :] = rate
        weights[table_rows(index), :] = norm_of(rate) * column_of(residue_ref, index)
        high, low = two_parts(jnp.exp(-rate * (lane + 1.0)) * in_first)
        both = dot(jnp.concatenate([high, low], axis=0), cotangent_ref[:, group(index)])
        spot = pl.ds(pl.multiple_of(8 + lax.rem(index, share) * modes, 8), modes)
        sens_out[index // share, spot, :] = both[:modes] + both[modes:]
        return carry

    depth = rows // PIECES

    def tagged(piece):
        return pl.ds(0, depth + 8) if piece == 0 else pl.ds(8 + piece * depth, depth)

    def sens_copy(piece, step, slot):
        target = lax.rem(mine + step, CLUSTER)
        return pltpu.make_async_remote_copy(
            src_ref=sens_out.at[target, tagged(piece)],
            dst_ref=sens_in.at[slot, tagged(piece)],
            send_sem=sens_send.at[piece, step],
            recv_sem=sens_recv.at[piece, slot],
            device_id={"ctx": home + target},
            device_id_type=MESH,
        )

    def sender_of(step):
        return lax.rem(mine + CLUSTER - step, CLUSTER)

    for part in range(CLUSTER):
        sens_out[part, :8, :] = tag
    fetches[3].wait()
    batch = share // PIECES
    for piece in range(PIECES):
        for turn, step in enumerate((2, 1, 3, 0)):
            base = lax.rem(mine + step, CLUSTER) * share + piece * batch
            for index in range(batch):
                sense(base + index, 0)
            if piece == 0 and turn == 0:
                pl.semaphore_wait(barrier, near_count + clusters - 2)
            if step:
                sens_copy(piece, step, mine).start()
        sens_in[mine, tagged(piece), :] = sens_out[mine, tagged(piece), :]
    fetches[4].wait()

    def inner(index, carry):
        rate = rates[table_rows(index), :]
        weight = weights[table_rows(index), :]
        tokens = signal_ref[:, group(index)]
        grads = cotangent_ref[:, group(index)]
        decay = jnp.exp(-rate * lane)
        lags = jnp.sum(weight * decay, axis=0, keepdims=True)
        spread = pltpu.roll(
            jnp.broadcast_to(lags, (length, length)), 0, 1, stride=1, stride_axis=0
        )
        linked = mask[...]
        local[:, group(index)] = dot((spread * linked).astype(BF16), grads)
        turned = dot(flip[...], tokens).astype(BF16)
        products = dot(turned, grads, ((1,), (1,))) * flipped_mask[...]
        aligned = pltpu.roll(products, 1, 1, stride=1, stride_axis=0)
        intra[table_rows(index), :] = jnp.sum(aligned, axis=0, keepdims=True) * decay
        high, low = two_parts(jnp.exp(-rate * (length - 1.0 - lane)) * in_last)
        both = dot(jnp.concatenate([high, low], axis=0), tokens)
        ends[table_rows(index), :] = both[:modes] + both[modes:]
        return carry

    shares = [filters * turn // (3 * PIECES) for turn in range(3 * PIECES + 1)]

    def advance(turn, until):
        lax.fori_loop(shares[turn], shares[until], inner, 0, unroll=2)

    def powers(piece):
        start = pl.multiple_of(mine * rows + piece * depth, 8)
        power = [None, jnp.exp(-rates[pl.ds(start, depth), :] * float(length))]
        for exponent in range(2, 2 * CLUSTER):
            power.append(power[exponent // 2] * power[exponent - exponent // 2])
        return power

    def times(power, exponent, value):
        return value if exponent == 0 else power[exponent] * value

    def sum_copy(piece, back):
        return pltpu.make_async_remote_copy(
            src_ref=sum_out.at[tagged(piece)],
            dst_ref=sum_in.at[back - 1, tagged(piece)],
            send_sem=sum_send.at[piece, back - 1],
            recv_sem=sum_recv.at[piece, back - 1],
            device_id={"ctx": me - back * CLUSTER},
            device_id_type=MESH,
        )

    def adj_copy(piece, step, slot):
        target = lax.rem(mine + step, CLUSTER)
        span = pl.ds(piece * depth, depth)
        return pltpu.make_async_remote_copy(
            src_ref=adj_out.at[target, span],
            dst_ref=adj_in.at[slot, span],
            send_sem=adj_send.at[piece, step],
            recv_sem=adj_recv.at[piece, slot],
            device_id={"ctx": home + target},
            device_id_type=MESH,
        )

    for back in (1, 2):

        @pl.when(me + back * CLUSTER >= shards)
        def _(back=back):
            sum_in[back - 1] = jnp.full(sum_in.shape[1:], -1.0, F32)

    for piece in range(PIECES):
        for step in range(1, CLUSTER):
            sens_copy(piece, step, sender_of(step)).wait_recv()
        power = powers(piece)
        firsts = [sens_in[place, 0:1, :] for place in range(CLUSTER)]
        lasts = [sens_in[place, 1:2, :] for place in range(CLUSTER)]
        span = pl.ds(8 + piece * depth, depth)
        sens = [sens_in[place, span, :] for place in range(CLUSTER)]
        total = sens[0]
        for place in range(1, CLUSTER):
            linked = jnp.where(firsts[place] == firsts[0], sens[place], 0.0)
            total = total + times(power, place, linked)
        sum_out[span, :] = total
        if piece == 0:
            sum_out[:8, :] = sens_in[0, :8, :]
        for back in (1, 2):

            @pl.when(me - back * CLUSTER >= 0)
            def _(piece=piece, back=back):
                sum_copy(piece, back).start()

        for place in range(CLUSTER):
            value = jnp.zeros((depth, width), F32)
            for later in range(place + 1, CLUSTER):
                linked = jnp.where(firsts[later] == lasts[place], sens[later], 0.0)
                value = value + times(power, later - place - 1, linked)
            adj_out[place, piece * depth : (piece + 1) * depth, :] = value
        advance(piece, piece + 1)

    for piece in range(PIECES):
        for back in (1, 2):

            @pl.when(me + back * CLUSTER < shards)
            def _(piece=piece, back=back):
                sum_copy(piece, back).wait_recv()

        power = powers(piece)
        part = slice(piece * depth, (piece + 1) * depth)
        span = pl.ds(8 + piece * depth, depth)
        for place in range(CLUSTER):
            value = adj_out[place, part, :]
            for back in (1, 2):
                hit = sum_in[back - 1, 0:1, :] == sens_in[place, 1:2, :]
                linked = jnp.where(hit, sum_in[back - 1, span, :], 0.0)
                value = value + times(power, back * CLUSTER - 1 - place, linked)
            adj_out[place, part, :] = value
        for step in (2, 1, 3):
            adj_copy(piece, step, mine).start()
        adj_in[mine, part, :] = adj_out[mine, part, :]
        advance(PIECES + piece, PIECES + piece + 1)

    advance(2 * PIECES, 3 * PIECES)
    for piece in range(PIECES):
        for step in range(1, CLUSTER):
            adj_copy(piece, step, sender_of(step)).wait_recv()

    def adjoint_of(index):
        spot = pl.ds(pl.multiple_of(lax.rem(index, share) * modes, modes), modes)
        return adj_in[index // share, spot, :]

    def account(index, terms):
        product = intra[table_rows(index), :] + ends[table_rows(index), :] * adjoint_of(index)
        term = jnp.sum(product, axis=1, keepdims=True)
        return jnp.where(filter_lane == index, term, terms)

    terms = lax.fori_loop(0, filters, account, jnp.zeros((modes, filters), F32), unroll=8)
    near_out[0] = norm_of(rate_ref[...]) * terms * scale

    def near_copy(step):
        return pltpu.make_async_remote_copy(
            src_ref=near_out.at[0],
            dst_ref=near_in.at[near_mine],
            send_sem=near_send.at[step],
            recv_sem=near_recv.at[near_mine],
            device_id=near_spot(step),
            device_id_type=MESH,
        )

    def near_arrival(step):
        sender = lax.rem(near_mine + near_count - step, near_count)
        return pltpu.make_async_remote_copy(
            src_ref=near_out.at[0],
            dst_ref=near_in.at[sender],
            send_sem=near_send.at[step],
            recv_sem=near_recv.at[sender],
            device_id=near_spot(step),
            device_id_type=MESH,
        )

    def far_copy(step):
        return pltpu.make_async_remote_copy(
            src_ref=near_out.at[1],
            dst_ref=far_in.at[block],
            send_sem=far_send.at[step],
            recv_sem=far_recv.at[block],
            device_id=far_spot(step),
            device_id_type=MESH,
        )

    def far_arrival(step):
        sender = lax.rem(block + clusters - step, clusters)
        return pltpu.make_async_remote_copy(
            src_ref=near_out.at[1],
            dst_ref=far_in.at[sender],
            send_sem=far_send.at[step],
            recv_sem=far_recv.at[sender],
            device_id=far_spot(step),
            device_id_type=MESH,
        )

    for step in range(1, near_count):
        near_copy(step).start()
    near_in[near_mine] = near_out[0]

    def finish(index, carry):
        rate = rates[table_rows(index), :]
        high, low = two_parts(jnp.exp(-rate * (length - 1.0 - lane)) * in_last)
        adj_high, adj_low = two_parts(weights[table_rows(index), :] * adjoint_of(index))
        left = jnp.concatenate([high, low, high], axis=0)
        right = jnp.concatenate([adj_high, adj_high, adj_low], axis=0)
        carried = dot(left, right, ((0,), (0,)))
        grad_ref[:, group(index)] = (local[:, group(index)] + carried).astype(BF16)
        return carry

    lax.fori_loop(0, filters // 2, finish, 0, unroll=4)
    for step in range(1, near_count):
        near_arrival(step).wait_recv()
    near_total = near_in[0]
    for rank in range(1, near_count):
        near_total = near_total + near_in[rank]
    near_out[1] = near_total
    for step in range(1, clusters):
        far_copy(step).start()
    far_in[block] = near_total
    lax.fori_loop(filters // 2, filters, finish, 0, unroll=4)
    for step in range(1, clusters):
        far_arrival(step).wait_recv()
    far_total = far_in[0]
    for rank in range(1, clusters):
        far_total = far_total + far_in[rank]
    term_ref[...] = far_total

    for step in range(1, near_count):
        near_copy(step).wait_send()
    for step in range(1, clusters):
        far_copy(step).wait_send()
    for piece in range(PIECES):
        for step in range(1, CLUSTER):
            sens_copy(piece, step, mine).wait_send()
            adj_copy(piece, step, mine).wait_send()
        for back in (1, 2):

            @pl.when(me - back * CLUSTER >= 0)
            def _(piece=piece, back=back):
                sum_copy(piece, back).wait_send()


def store(grad_ref, term_ref, grad_hbm, term_hbm, sems):
    copies = [
        pltpu.make_async_copy(term_ref, term_hbm, sems.at[0]),
        pltpu.make_async_copy(grad_ref, grad_hbm, sems.at[1]),
    ]
    for copy in copies:
        copy.start()
    for copy in copies:
        copy.wait()


def body(signal, cotangent, record_id, rate, residue):
    length, width = signal.shape[1:]
    filters, modes = rate.shape
    shards = lax.axis_size("ctx")
    group_width = width // filters
    rows = filters // CLUSTER * modes
    sequences = signal.shape[0] * lax.axis_size("dp")
    scale = 1.0 / math.sqrt(sequences * length * shards * group_width)
    copies = lax.axis_size("dp")
    near_count = CLUSTER * copies
    clusters = shards // CLUSTER
    vmem = pl.BlockSpec(memory_space=pltpu.VMEM)
    in_hbm = functools.partial(pltpu.with_memory_space_constraint, memory_space=pltpu.HBM)
    dma = pltpu.SemaphoreType.DMA
    grad, terms = pl.pallas_call(
        functools.partial(kernel, filters, modes, shards, scale, copies),
        out_shape=(pltpu.VMEM((length, width), BF16), pltpu.VMEM((modes, filters), F32)),
        in_specs=[pl.BlockSpec(memory_space=pltpu.HBM)] * 5,
        out_specs=(vmem, vmem),
        scratch_shapes=[
            pltpu.VMEM((length, width), BF16),
            pltpu.VMEM((length, width), BF16),
            pltpu.VMEM(record_id.shape, jnp.int32),
            pltpu.VMEM((modes, filters), F32),
            pltpu.VMEM((modes, filters), F32),
            pltpu.VMEM((filters * modes, group_width), F32),
            pltpu.VMEM((filters * modes, group_width), F32),
            pltpu.VMEM((length, length), F32),
            pltpu.VMEM((length, length), BF16),
            pltpu.VMEM((length, length), F32),
            pltpu.VMEM((length, width), F32),
            pltpu.VMEM((filters * modes, group_width), F32),
            pltpu.VMEM((filters * modes, group_width), F32),
            pltpu.VMEM((CLUSTER, rows + 8, group_width), F32),
            pltpu.VMEM((CLUSTER, rows + 8, group_width), F32),
            pltpu.VMEM((rows + 8, group_width), F32),
            pltpu.VMEM((2, rows + 8, group_width), F32),
            pltpu.VMEM((CLUSTER, rows, group_width), F32),
            pltpu.VMEM((CLUSTER, rows, group_width), F32),
            dma((PIECES, CLUSTER)),
            dma((PIECES, CLUSTER)),
            dma((PIECES, 2)),
            dma((PIECES, 2)),
            dma((PIECES, CLUSTER)),
            dma((PIECES, CLUSTER)),
            pltpu.VMEM((2, modes, filters), F32),
            pltpu.VMEM((near_count, modes, filters), F32),
            pltpu.VMEM((clusters, modes, filters), F32),
            dma((near_count,)),
            dma((near_count,)),
            dma((clusters,)),
            dma((clusters,)),
            dma((5,)),
        ],
        compiler_params=pltpu.CompilerParams(
            collective_id=0, has_side_effects=True, vmem_limit_bytes=52 << 20
        ),
    )(*(in_hbm(x) for x in (signal[0], cotangent[0], record_id, rate.T, residue.T)))
    grad, terms = pl.pallas_call(
        store,
        out_shape=(
            jax.ShapeDtypeStruct((length, width), BF16),
            jax.ShapeDtypeStruct((modes, filters), F32),
        ),
        in_specs=[vmem, vmem],
        out_specs=(pl.BlockSpec(memory_space=pltpu.HBM), pl.BlockSpec(memory_space=pltpu.HBM)),
        scratch_shapes=[dma((2,))],
    )(*(pltpu.with_memory_space_constraint(x, pltpu.VMEM) for x in (grad, terms)))
    return grad[None], terms.T


def solution(mesh):
    return jax.shard_map(
        body,
        mesh=mesh,
        in_specs=(P("dp", "ctx", None), P("dp", "ctx", None), P("dp", "ctx"), P(), P()),
        out_specs=(P("dp", "ctx", None), P()),
        check_vma=False,
    )
```

```python
import functools
import math

import jax
import jax.numpy as jnp
from jax import lax
from jax.experimental import pallas as pl
from jax.experimental.pallas import tpu as pltpu
from jax.sharding import PartitionSpec as P

CLUSTER = 4
PIECES = 4
BACKS = (1, 2)
MESH = pl.DeviceIdType.MESH
F32 = jnp.float32
BF16 = jnp.bfloat16


def two_parts(table):
    high = table.astype(BF16)
    return high, (table - high.astype(F32)).astype(BF16)


def dot(left, right, contract=((1,), (0,))):
    return lax.dot_general(left, right, (contract, ((), ())), preferred_element_type=F32)


def kernel(
    filters,
    modes,
    shards,
    scale,
    copies,
    signal_hbm,
    cotangent_hbm,
    record_hbm,
    rate_hbm,
    residue_hbm,
    grad_ref,
    term_ref,
    signal_ref,
    cotangent_ref,
    record_ref,
    rate_ref,
    residue_ref,
    rates,
    weights,
    mask,
    edges,
    local,
    sens_out,
    sens_in,
    ends_out,
    ends_in,
    sum_out,
    sum_in,
    adj_out,
    adj_in,
    near_out,
    near_in,
    far_in,
    send_sem,
    sum_send,
    sens_recv,
    ends_recv,
    sum_recv,
    adj_recv,
    reduce_recv,
    fetch_sem,
):
    length = signal_ref.shape[0]
    width = signal_ref.shape[1] // filters
    share = filters // CLUSTER
    rows = share * modes
    depth = rows // PIECES
    batch = share // PIECES
    me = lax.axis_index("ctx")
    mine = lax.rem(me, CLUSTER)
    home = me - mine
    clusters = shards // CLUSTER
    block = me // CLUSTER
    copy_of = lax.axis_index("dp")
    near_count = CLUSTER * copies
    near_mine = copy_of * CLUSTER + mine
    to_sens, to_ends, to_adj, to_near, to_far = range(5)

    def near_spot(step):
        rank = lax.rem(near_mine + step, near_count)
        return {"ctx": home + lax.rem(rank, CLUSTER), "dp": rank // CLUSTER}

    def far_spot(step):
        return {"ctx": lax.rem(block + step, clusters) * CLUSTER + mine, "dp": copy_of}

    fetches = [
        pltpu.make_async_copy(source, target, fetch_sem.at[place])
        for place, (source, target) in enumerate(
            (
                (record_hbm, record_ref),
                (rate_hbm, rate_ref),
                (residue_hbm, residue_ref),
                (cotangent_hbm, cotangent_ref),
                (signal_hbm, signal_ref),
            )
        )
    ]
    for fetch in fetches:
        fetch.start()
    barrier = pltpu.get_barrier_semaphore()
    for step in range(1, near_count):
        pl.semaphore_signal(barrier, inc=1, device_id=near_spot(step), device_id_type=MESH)
    for step in range(1, clusters):
        pl.semaphore_signal(barrier, inc=1, device_id=far_spot(step), device_id_type=MESH)

    lane = lax.broadcasted_iota(jnp.int32, (modes, length), 1).astype(F32)
    filter_lane = lax.broadcasted_iota(jnp.int32, (modes, filters), 1)
    tag_row = lax.broadcasted_iota(jnp.int32, (8, width), 0)
    row = lax.broadcasted_iota(jnp.int32, (length, length), 0)
    column = lax.broadcasted_iota(jnp.int32, (length, length), 1)
    for fetch in fetches[:3]:
        fetch.wait()
    ids = jnp.broadcast_to(record_ref[...].astype(F32), (length, length))
    first = ids[:8, :1]
    last = ids[:8, length - 1 :]
    in_first = (ids[:1] == first[:1]).astype(F32)
    in_last = (ids[:1] == last[:1]).astype(F32)
    mask[...] = jnp.where((ids == ids.T) & (column >= row), 1.0, 0.0)
    tag = jnp.where(tag_row == 0, first, last)

    def group(index):
        return pl.ds(pl.multiple_of(index * width, width), width)

    def table_rows(index):
        return pl.ds(pl.multiple_of(index * modes, modes), modes)

    def edge_rows(index):
        return pl.ds(pl.multiple_of(index * 2 * modes, 2 * modes), 2 * modes)

    def column_of(ref, index):
        return jnp.sum(jnp.where(filter_lane == index, ref[...], 0.0), axis=1, keepdims=True)

    def norm_of(rate):
        double = 2.0 * rate
        series = 1.0 - double * (1.0 / 6.0) * (1.0 - double * (1.0 / 7.0))
        for divisor in (5.0, 4.0, 3.0, 2.0):
            series = 1.0 - double * (1.0 / divisor) * series
        return jnp.sqrt(double * series)

    def tagged(piece):
        return pl.ds(0, depth + 8) if piece == 0 else pl.ds(8 + piece * depth, depth)

    def plain(piece):
        return pl.ds(piece * depth, depth)

    def to_peer(source, target, send, recv, step):
        return pltpu.make_async_remote_copy(
            src_ref=source,
            dst_ref=target,
            send_sem=send_sem.at[send],
            recv_sem=recv,
            device_id={"ctx": home + lax.rem(mine + step, CLUSTER)},
            device_id_type=MESH,
        )

    def sens_copy(piece, step):
        peer = lax.rem(mine + step, CLUSTER)
        return to_peer(
            sens_out.at[peer, tagged(piece)],
            sens_in.at[mine, tagged(piece)],
            to_sens,
            sens_recv.at[piece],
            step,
        )

    def ends_copy(piece, step):
        peer = lax.rem(mine + step, CLUSTER)
        return to_peer(
            ends_out.at[peer, plain(piece)],
            ends_in.at[mine, plain(piece)],
            to_ends,
            ends_recv.at[0],
            step,
        )

    def adj_copy(piece, step):
        peer = lax.rem(mine + step, CLUSTER)
        return to_peer(
            adj_out.at[peer, plain(piece)],
            adj_in.at[mine, plain(piece)],
            to_adj,
            adj_recv.at[piece],
            step,
        )

    def wait_peers(ref, span, send, recv):
        several = ref.at[pl.ds(0, CLUSTER - 1), span]
        to_peer(several, several, send, recv, 1).wait_recv()

    def wait_sent(ref, send):
        several = ref.at[pl.ds(0, CLUSTER - 1)]
        to_peer(several, several, send, ends_recv.at[0], 1).wait_send()

    def sum_copy(piece, back):
        return pltpu.make_async_remote_copy(
            src_ref=sum_out.at[tagged(piece)],
            dst_ref=sum_in.at[back - 1, tagged(piece)],
            send_sem=sum_send.at[back - 1],
            recv_sem=sum_recv.at[piece, back - 1],
            device_id={"ctx": me - back * CLUSTER},
            device_id_type=MESH,
        )

    def sense(index):
        rate = jnp.broadcast_to(column_of(rate_ref, index), (modes, width))
        rates[table_rows(index), :] = rate
        weights[table_rows(index), :] = norm_of(rate) * column_of(residue_ref, index)
        high, low = two_parts(jnp.exp(-rate * (lane + 1.0)) * in_first)
        both = dot(jnp.concatenate([high, low], axis=0), cotangent_ref[:, group(index)])
        spot = pl.ds(pl.multiple_of(8 + lax.rem(index, share) * modes, 8), modes)
        sens_out[index // share, spot, :] = both[:modes] + both[modes:]

    def end(index):
        rate = rates[table_rows(index), :]
        high, low = two_parts(jnp.exp(-rate * (length - 1.0 - lane)) * in_last)
        pair = jnp.concatenate([high, low], axis=0)
        edges[edge_rows(index), :] = pair
        both = dot(pair, signal_ref[:, group(index)])
        spot = pl.ds(pl.multiple_of(lax.rem(index, share) * modes, modes), modes)
        ends_out[index // share, spot, :] = both[:modes] + both[modes:]

    row_of = lax.broadcasted_iota(jnp.int32, (8, length), 0)

    def intra(index, terms):
        rate = rates[table_rows(index), :]
        products = dot(signal_ref[:, group(index)], cotangent_ref[:, group(index)], ((1,), (1,)))
        products = products * mask[...]
        parts = [products[:8]]
        for start in range(8, length, 8):
            parts.append(pltpu.roll(products[start : start + 8], length - start, 1))
        while len(parts) > 1:
            parts = [parts[i] + parts[i + 1] for i in range(0, len(parts), 2)]
        by_lag = parts[0]
        for bit in (1, 2, 4):
            moved = pltpu.roll(by_lag, length - bit, 1)
            by_lag = jnp.where((row_of & bit) != 0, moved, by_lag)
        by_lag = jnp.sum(by_lag, axis=0, keepdims=True)
        term = jnp.sum(by_lag * jnp.exp(-rate * lane), axis=1, keepdims=True)
        return jnp.where(filter_lane == index, term, terms)

    def near_by(index, carry):
        rate = rates[table_rows(index), :]
        weight = weights[table_rows(index), :]
        lags = jnp.sum(weight * jnp.exp(-rate * lane), axis=0, keepdims=True)
        spread = pltpu.roll(
            jnp.broadcast_to(lags, (length, length)), 0, 1, stride=1, stride_axis=0
        )
        kernel_now = (spread * mask[...]).astype(BF16)
        local[:, group(index)] = dot(kernel_now, cotangent_ref[:, group(index)])
        return carry

    for part in range(CLUSTER):
        sens_out[part, :8, :] = tag
    for back in BACKS:

        @pl.when(me + back * CLUSTER >= shards)
        def _(back=back):
            sum_in[back - 1] = jnp.full(sum_in.shape[1:], -1.0, F32)

    fetches[3].wait()
    for piece in range(PIECES):
        for turn, step in enumerate((2, 1, 3, 0)):
            base = lax.rem(mine + step, CLUSTER) * share + piece * batch
            for index in range(batch):
                sense(base + index)
            if piece == 0 and turn == 0:
                pl.semaphore_wait(barrier, near_count + clusters - 2)
            if step:
                sens_copy(piece, step).start()
        sens_in[mine, tagged(piece), :] = sens_out[mine, tagged(piece), :]
    fetches[4].wait()
    for piece in range(PIECES):
        for step in (2, 1, 3, 0):
            base = lax.rem(mine + step, CLUSTER) * share + piece * batch
            for index in range(batch):
                end(base + index)
            if step:
                ends_copy(piece, step).start()
        ends_in[mine, plain(piece), :] = ends_out[mine, plain(piece), :]

    def powers(piece):
        start = pl.multiple_of(mine * rows + piece * depth, 8)
        power = [None, jnp.exp(-rates[pl.ds(start, depth), :] * float(length))]
        for exponent in range(2, 2 * CLUSTER):
            power.append(power[exponent // 2] * power[exponent - exponent // 2])
        return power

    def times(power, exponent, value):
        return value if exponent == 0 else power[exponent] * value

    terms = jnp.zeros((modes, filters), F32)
    terms = lax.fori_loop(0, 16, intra, terms, unroll=16)

    for piece in range(PIECES):
        wait_peers(sens_in, tagged(piece), to_sens, sens_recv.at[piece])
        power = powers(piece)
        firsts = [sens_in[place, 0:1, :] for place in range(CLUSTER)]
        lasts = [sens_in[place, 1:2, :] for place in range(CLUSTER)]
        span = pl.ds(8 + piece * depth, depth)
        sens = [sens_in[place, span, :] for place in range(CLUSTER)]
        total = sens[0]
        for place in range(1, CLUSTER):
            linked = jnp.where(firsts[place] == firsts[0], sens[place], 0.0)
            total = total + times(power, place, linked)
        sum_out[span, :] = total
        if piece == 0:
            sum_out[:8, :] = sens_in[0, :8, :]
        for back in BACKS:

            @pl.when(me - back * CLUSTER >= 0)
            def _(piece=piece, back=back):
                sum_copy(piece, back).start()

        for place in range(CLUSTER):
            value = jnp.zeros((depth, width), F32)
            for later in range(place + 1, CLUSTER):
                linked = jnp.where(firsts[later] == lasts[place], sens[later], 0.0)
                value = value + times(power, later - place - 1, linked)
            adj_out[place, plain(piece), :] = value

    terms = lax.fori_loop(16, filters, intra, terms, unroll=16)

    for piece in range(PIECES):
        for back in BACKS:

            @pl.when(me + back * CLUSTER < shards)
            def _(piece=piece, back=back):
                sum_copy(piece, back).wait_recv()

        power = powers(piece)
        span = pl.ds(8 + piece * depth, depth)
        for place in range(CLUSTER):
            value = adj_out[place, plain(piece), :]
            for back in BACKS:
                hit = sum_in[back - 1, 0:1, :] == sens_in[place, 1:2, :]
                linked = jnp.where(hit, sum_in[back - 1, span, :], 0.0)
                value = value + times(power, back * CLUSTER - 1 - place, linked)
            adj_out[place, plain(piece), :] = value
        for step in (2, 1, 3):
            adj_copy(piece, step).start()
        adj_in[mine, plain(piece), :] = adj_out[mine, plain(piece), :]

    wait_peers(ends_in, pl.ds(0, rows), to_ends, ends_recv.at[0])
    product = ends_in[0] * adj_out[0]
    for place in range(1, CLUSTER):
        product = product + ends_in[place] * adj_out[place]
    carried = jnp.sum(product, axis=1, keepdims=True)
    for index in range(share):
        hit = filter_lane == mine * share + index
        terms = terms + jnp.where(hit, carried[index * modes : (index + 1) * modes], 0.0)
    near_out[0] = norm_of(rate_ref[...]) * terms * scale

    def near_copy(step):
        return pltpu.make_async_remote_copy(
            src_ref=near_out.at[0],
            dst_ref=near_in.at[near_mine],
            send_sem=send_sem.at[to_near],
            recv_sem=reduce_recv.at[0],
            device_id=near_spot(step),
            device_id_type=MESH,
        )

    def far_copy(step):
        return pltpu.make_async_remote_copy(
            src_ref=near_out.at[1],
            dst_ref=far_in.at[block],
            send_sem=send_sem.at[to_far],
            recv_sem=reduce_recv.at[1],
            device_id=far_spot(step),
            device_id_type=MESH,
        )

    def all_of(ref, count, send, recv):
        several = ref.at[pl.ds(0, count)]
        return to_peer(several, several, send, recv, 1)

    near_all = all_of(near_in, near_count - 1, to_near, reduce_recv.at[0])
    far_all = all_of(far_in, clusters - 1, to_far, reduce_recv.at[1])

    for step in range(1, near_count):
        near_copy(step).start()
    near_in[near_mine] = near_out[0]

    lax.fori_loop(0, filters, near_by, 0, unroll=16)

    near_all.wait_recv()
    near_total = near_in[0]
    for rank in range(1, near_count):
        near_total = near_total + near_in[rank]
    near_out[1] = near_total
    for step in range(1, clusters):
        far_copy(step).start()
    far_in[block] = near_total

    def finish(index):
        high_low = edges[edge_rows(index), :]
        spot = pl.ds(pl.multiple_of(lax.rem(index, share) * modes, modes), modes)
        adjoint = adj_in[index // share, spot, :]
        adj_high, adj_low = two_parts(weights[table_rows(index), :] * adjoint)
        left = jnp.concatenate([high_low, high_low[:modes]], axis=0)
        right = jnp.concatenate([adj_high, adj_high, adj_low], axis=0)
        carried = dot(left, right, ((0,), (0,)))
        grad_ref[:, group(index)] = (local[:, group(index)] + carried).astype(BF16)

    for piece in range(PIECES):
        wait_peers(adj_in, plain(piece), to_adj, adj_recv.at[piece])

        def finish_one(turn, carry, piece=piece):
            finish(turn // batch * share + piece * batch + lax.rem(turn, batch))
            return carry

        lax.fori_loop(0, CLUSTER * batch, finish_one, 0, unroll=8)

    far_all.wait_recv()
    far_total = far_in[0]
    for rank in range(1, clusters):
        far_total = far_total + far_in[rank]
    term_ref[...] = far_total

    wait_sent(sens_out, to_sens)
    wait_sent(ends_out, to_ends)
    wait_sent(adj_out, to_adj)
    near_all.wait_send()
    far_all.wait_send()
    for back in BACKS:

        @pl.when(me - back * CLUSTER >= 0)
        def _(back=back):
            pltpu.make_async_remote_copy(
                src_ref=sum_out,
                dst_ref=sum_in.at[back - 1],
                send_sem=sum_send.at[back - 1],
                recv_sem=sum_recv.at[0, back - 1],
                device_id={"ctx": me - back * CLUSTER},
                device_id_type=MESH,
            ).wait_send()


def store(grad_ref, term_ref, grad_hbm, term_hbm, sems):
    copies = [
        pltpu.make_async_copy(term_ref, term_hbm, sems.at[0]),
        pltpu.make_async_copy(grad_ref, grad_hbm, sems.at[1]),
    ]
    for copy in copies:
        copy.start()
    for copy in copies:
        copy.wait()


def body(signal, cotangent, record_id, rate, residue):
    length, width = signal.shape[1:]
    filters, modes = rate.shape
    shards = lax.axis_size("ctx")
    group_width = width // filters
    rows = filters // CLUSTER * modes
    sequences = signal.shape[0] * lax.axis_size("dp")
    scale = 1.0 / math.sqrt(sequences * length * shards * group_width)
    copies = lax.axis_size("dp")
    near_count = CLUSTER * copies
    clusters = shards // CLUSTER
    hbm = pl.BlockSpec(memory_space=pltpu.HBM)
    vmem = pl.BlockSpec(memory_space=pltpu.VMEM)
    in_hbm = functools.partial(pltpu.with_memory_space_constraint, memory_space=pltpu.HBM)
    in_vmem = functools.partial(pltpu.with_memory_space_constraint, memory_space=pltpu.VMEM)
    dma = pltpu.SemaphoreType.DMA
    grad, terms = pl.pallas_call(
        functools.partial(kernel, filters, modes, shards, scale, copies),
        out_shape=(pltpu.VMEM((length, width), BF16), pltpu.VMEM((modes, filters), F32)),
        in_specs=[hbm] * 5,
        out_specs=(vmem, vmem),
        scratch_shapes=[
            pltpu.VMEM((length, width), BF16),
            pltpu.VMEM((length, width), BF16),
            pltpu.VMEM(record_id.shape, jnp.int32),
            pltpu.VMEM((modes, filters), F32),
            pltpu.VMEM((modes, filters), F32),
            pltpu.VMEM((filters * modes, group_width), F32),
            pltpu.VMEM((filters * modes, group_width), F32),
            pltpu.VMEM((length, length), F32),
            pltpu.VMEM((filters * 2 * modes, length), BF16),
            pltpu.VMEM((length, width), F32),
            pltpu.VMEM((CLUSTER, rows + 8, group_width), F32),
            pltpu.VMEM((CLUSTER, rows + 8, group_width), F32),
            pltpu.VMEM((CLUSTER, rows, group_width), F32),
            pltpu.VMEM((CLUSTER, rows, group_width), F32),
            pltpu.VMEM((rows + 8, group_width), F32),
            pltpu.VMEM((2, rows + 8, group_width), F32),
            pltpu.VMEM((CLUSTER, rows, group_width), F32),
            pltpu.VMEM((CLUSTER, rows, group_width), F32),
            pltpu.VMEM((2, modes, filters), F32),
            pltpu.VMEM((near_count, modes, filters), F32),
            pltpu.VMEM((clusters, modes, filters), F32),
            dma((5,)),
            dma((2,)),
            dma((PIECES,)),
            dma((1,)),
            dma((PIECES, 2)),
            dma((PIECES,)),
            dma((2,)),
            dma((5,)),
        ],
        compiler_params=pltpu.CompilerParams(
            collective_id=0, has_side_effects=True, vmem_limit_bytes=52 << 20
        ),
    )(*(in_hbm(x) for x in (signal[0], cotangent[0], record_id, rate.T, residue.T)))
    grad, terms = pl.pallas_call(
        store,
        out_shape=(
            jax.ShapeDtypeStruct((length, width), BF16),
            jax.ShapeDtypeStruct((modes, filters), F32),
        ),
        in_specs=[vmem, vmem],
        out_specs=(hbm, hbm),
        scratch_shapes=[dma((2,))],
    )(in_vmem(grad), in_vmem(terms))
    return grad[None], terms.T


def solution(mesh):
    return jax.shard_map(
        body,
        mesh=mesh,
        in_specs=(P("dp", "ctx", None), P("dp", "ctx", None), P("dp", "ctx"), P(), P()),
        out_specs=(P("dp", "ctx", None), P()),
        check_vma=False,
    )
```

```python
import functools
import math

import jax
import jax.numpy as jnp
from jax import lax
from jax.experimental import pallas as pl
from jax.experimental.pallas import tpu as pltpu
from jax.sharding import PartitionSpec as P

CLUSTER = 4
PIECES = 4
BACKS = (1, 2)
MESH = pl.DeviceIdType.MESH
F32 = jnp.float32
BF16 = jnp.bfloat16


def two_parts(table):
    high = table.astype(BF16)
    return high, (table - high.astype(F32)).astype(BF16)


def dot(left, right, contract=((1,), (0,))):
    return lax.dot_general(left, right, (contract, ((), ())), preferred_element_type=F32)


def kernel(
    filters,
    modes,
    shards,
    scale,
    copies,
    signal_hbm,
    cotangent_hbm,
    record_hbm,
    rate_hbm,
    residue_hbm,
    grad_ref,
    term_ref,
    signal_ref,
    cotangent_ref,
    record_ref,
    rate_ref,
    residue_ref,
    rates,
    weights,
    mask,
    edges,
    local,
    sens_out,
    sens_in,
    ends_out,
    ends_in,
    sum_out,
    sum_in,
    adj_out,
    adj_in,
    near_out,
    near_in,
    far_in,
    send_sem,
    sum_send,
    sens_recv,
    ends_recv,
    sum_recv,
    adj_recv,
    reduce_recv,
    fetch_sem,
):
    length = signal_ref.shape[0]
    width = signal_ref.shape[1] // filters
    share = filters // CLUSTER
    rows = share * modes
    depth = rows // PIECES
    batch = share // PIECES
    me = lax.axis_index("ctx")
    mine = lax.rem(me, CLUSTER)
    home = me - mine
    clusters = shards // CLUSTER
    block = me // CLUSTER
    copy_of = lax.axis_index("dp")
    near_count = CLUSTER * copies
    near_mine = copy_of * CLUSTER + mine
    to_sens, to_ends, to_adj, to_near, to_far = range(5)

    def near_spot(step):
        rank = lax.rem(near_mine + step, near_count)
        return {"ctx": home + lax.rem(rank, CLUSTER), "dp": rank // CLUSTER}

    def far_spot(step):
        return {"ctx": lax.rem(block + step, clusters) * CLUSTER + mine, "dp": copy_of}

    fetches = [
        pltpu.make_async_copy(source, target, fetch_sem.at[place])
        for place, (source, target) in enumerate(
            (
                (record_hbm, record_ref),
                (rate_hbm, rate_ref),
                (residue_hbm, residue_ref),
                (cotangent_hbm, cotangent_ref),
                (signal_hbm, signal_ref),
            )
        )
    ]
    for fetch in fetches:
        fetch.start()
    barrier = pltpu.get_barrier_semaphore()
    for step in range(1, near_count):
        pl.semaphore_signal(barrier, inc=1, device_id=near_spot(step), device_id_type=MESH)
    for step in range(1, clusters):
        pl.semaphore_signal(barrier, inc=1, device_id=far_spot(step), device_id_type=MESH)

    lane = lax.broadcasted_iota(jnp.int32, (modes, length), 1).astype(F32)
    filter_lane = lax.broadcasted_iota(jnp.int32, (modes, filters), 1)
    tag_row = lax.broadcasted_iota(jnp.int32, (8, width), 0)
    row = lax.broadcasted_iota(jnp.int32, (length, length), 0)
    column = lax.broadcasted_iota(jnp.int32, (length, length), 1)
    for fetch in fetches[:3]:
        fetch.wait()
    ids = jnp.broadcast_to(record_ref[...].astype(F32), (length, length))
    first = ids[:8, :1]
    last = ids[:8, length - 1 :]
    in_first = (ids[:1] == first[:1]).astype(F32)
    in_last = (ids[:1] == last[:1]).astype(F32)
    tag = jnp.where(tag_row == 0, first, last)

    def group(index):
        return pl.ds(pl.multiple_of(index * width, width), width)

    def table_rows(index):
        return pl.ds(pl.multiple_of(index * modes, modes), modes)

    def edge_rows(index):
        return pl.ds(pl.multiple_of(index * 2 * modes, 2 * modes), 2 * modes)

    def column_of(ref, index):
        return jnp.sum(jnp.where(filter_lane == index, ref[...], 0.0), axis=1, keepdims=True)

    def norm_of(rate):
        double = 2.0 * rate
        series = 1.0 - double * (1.0 / 6.0) * (1.0 - double * (1.0 / 7.0))
        for divisor in (5.0, 4.0, 3.0, 2.0):
            series = 1.0 - double * (1.0 / divisor) * series
        return jnp.sqrt(double * series)

    def tagged(piece):
        return pl.ds(0, depth + 8) if piece == 0 else pl.ds(8 + piece * depth, depth)

    def plain(piece):
        return pl.ds(piece * depth, depth)

    def to_peer(source, target, send, recv, step):
        return pltpu.make_async_remote_copy(
            src_ref=source,
            dst_ref=target,
            send_sem=send_sem.at[send],
            recv_sem=recv,
            device_id={"ctx": home + lax.rem(mine + step, CLUSTER)},
            device_id_type=MESH,
        )

    def sens_copy(piece, step):
        peer = lax.rem(mine + step, CLUSTER)
        return to_peer(
            sens_out.at[peer, tagged(piece)],
            sens_in.at[mine, tagged(piece)],
            to_sens,
            sens_recv.at[piece],
            step,
        )

    def ends_copy(piece, step):
        peer = lax.rem(mine + step, CLUSTER)
        return to_peer(
            ends_out.at[peer, plain(piece)],
            ends_in.at[mine, plain(piece)],
            to_ends,
            ends_recv.at[0],
            step,
        )

    def adj_copy(piece, step):
        peer = lax.rem(mine + step, CLUSTER)
        return to_peer(
            adj_out.at[peer, plain(piece)],
            adj_in.at[mine, plain(piece)],
            to_adj,
            adj_recv.at[piece],
            step,
        )

    def wait_peers(ref, span, send, recv):
        several = ref.at[pl.ds(0, CLUSTER - 1), span]
        to_peer(several, several, send, recv, 1).wait_recv()

    def wait_sent(ref, send):
        several = ref.at[pl.ds(0, CLUSTER - 1)]
        to_peer(several, several, send, ends_recv.at[0], 1).wait_send()

    def sum_copy(piece, back):
        return pltpu.make_async_remote_copy(
            src_ref=sum_out.at[tagged(piece)],
            dst_ref=sum_in.at[back - 1, tagged(piece)],
            send_sem=sum_send.at[back - 1],
            recv_sem=sum_recv.at[piece, back - 1],
            device_id={"ctx": me - back * CLUSTER},
            device_id_type=MESH,
        )

    def sense(index):
        rate = jnp.broadcast_to(column_of(rate_ref, index), (modes, width))
        rates[table_rows(index), :] = rate
        weights[table_rows(index), :] = norm_of(rate) * column_of(residue_ref, index)
        high, low = two_parts(jnp.exp(-rate * (lane + 1.0)) * in_first)
        both = dot(jnp.concatenate([high, low], axis=0), cotangent_ref[:, group(index)])
        spot = pl.ds(pl.multiple_of(8 + lax.rem(index, share) * modes, 8), modes)
        sens_out[index // share, spot, :] = both[:modes] + both[modes:]

    def end(index):
        rate = rates[table_rows(index), :]
        high, low = two_parts(jnp.exp(-rate * (length - 1.0 - lane)) * in_last)
        pair = jnp.concatenate([high, low], axis=0)
        edges[edge_rows(index), :] = pair
        both = dot(pair, signal_ref[:, group(index)])
        spot = pl.ds(pl.multiple_of(lax.rem(index, share) * modes, modes), modes)
        ends_out[index // share, spot, :] = both[:modes] + both[modes:]

    row_of = lax.broadcasted_iota(jnp.int32, (8, length), 0)

    def intra(index, terms):
        rate = rates[table_rows(index), :]
        products = dot(signal_ref[:, group(index)], cotangent_ref[:, group(index)], ((1,), (1,)))
        products = products * mask[...]
        parts = [products[:8]]
        for start in range(8, length, 8):
            parts.append(pltpu.roll(products[start : start + 8], length - start, 1))
        while len(parts) > 1:
            parts = [parts[i] + parts[i + 1] for i in range(0, len(parts), 2)]
        by_lag = parts[0]
        for bit in (1, 2, 4):
            moved = pltpu.roll(by_lag, length - bit, 1)
            by_lag = jnp.where((row_of & bit) != 0, moved, by_lag)
        by_lag = jnp.sum(by_lag, axis=0, keepdims=True)
        term = jnp.sum(by_lag * jnp.exp(-rate * lane), axis=1, keepdims=True)
        return jnp.where(filter_lane == index, term, terms)

    def near_by(index, carry):
        rate = rates[table_rows(index), :]
        weight = weights[table_rows(index), :]
        lags = jnp.sum(weight * jnp.exp(-rate * lane), axis=0, keepdims=True)
        spread = pltpu.roll(
            jnp.broadcast_to(lags, (length, length)), 0, 1, stride=1, stride_axis=0
        )
        kernel_now = (spread * mask[...]).astype(BF16)
        local[:, group(index)] = dot(kernel_now, cotangent_ref[:, group(index)])
        return carry

    for part in range(CLUSTER):
        sens_out[part, :8, :] = tag
    for back in BACKS:

        @pl.when(me + back * CLUSTER >= shards)
        def _(back=back):
            sum_in[back - 1] = jnp.full(sum_in.shape[1:], -1.0, F32)

    fetches[3].wait()
    for piece in range(PIECES):
        for step in (2, 1, 3, 0):
            base = lax.rem(mine + step, CLUSTER) * share + piece * batch
            for index in range(batch):
                sense(base + index)
        if piece == 0:
            pl.semaphore_wait(barrier, near_count + clusters - 2)
        for step in (2, 1, 3):
            sens_copy(piece, step).start()
        sens_in[mine, tagged(piece), :] = sens_out[mine, tagged(piece), :]
    mask[...] = jnp.where((ids == ids.T) & (column >= row), 1.0, 0.0)
    fetches[4].wait()
    for piece in range(PIECES):
        for step in (2, 1, 3, 0):
            base = lax.rem(mine + step, CLUSTER) * share + piece * batch
            for index in range(batch):
                end(base + index)
    for piece in range(PIECES):
        for step in (2, 1, 3):
            ends_copy(piece, step).start()
        ends_in[mine, plain(piece), :] = ends_out[mine, plain(piece), :]

    def decay_of(piece):
        start = pl.multiple_of(mine * rows + piece * depth, 8)
        return jnp.exp(-rates[pl.ds(start, depth), :] * float(length))

    terms = jnp.zeros((modes, filters), F32)
    terms = lax.fori_loop(0, 16, intra, terms, unroll=16)

    for piece in range(PIECES):
        wait_peers(sens_in, tagged(piece), to_sens, sens_recv.at[piece])
        decay = decay_of(piece)
        firsts = [sens_in[place, 0:1, :] for place in range(CLUSTER)]
        lasts = [sens_in[place, 1:2, :] for place in range(CLUSTER)]
        span = pl.ds(8 + piece * depth, depth)
        values = []
        value = jnp.zeros((depth, width), F32)
        for place in range(CLUSTER - 1, -1, -1):
            values.append(value)
            value = jnp.where(firsts[place] == lasts[place], decay * value, 0.0)
            value = sens_in[place, span, :] + value
            if place:
                value = jnp.where(firsts[place] == lasts[place - 1], value, 0.0)
        sum_out[span, :] = value
        if piece == 0:
            sum_out[:8, :] = sens_in[0, :8, :]
        for back in BACKS:

            @pl.when(me - back * CLUSTER >= 0)
            def _(piece=piece, back=back):
                sum_copy(piece, back).start()

        for place, value in enumerate(reversed(values)):
            adj_out[place, plain(piece), :] = value

    terms = lax.fori_loop(16, filters, intra, terms, unroll=16)

    for piece in range(PIECES):
        for back in BACKS:

            @pl.when(me + back * CLUSTER < shards)
            def _(piece=piece, back=back):
                sum_copy(piece, back).wait_recv()

        decay = decay_of(piece)
        span = pl.ds(8 + piece * depth, depth)
        fourth = decay * decay
        fourth = fourth * fourth
        moved = [sum_in[0, span, :], fourth * sum_in[1, span, :]]
        for place in range(CLUSTER - 1, -1, -1):
            value = adj_out[place, plain(piece), :]
            for back in BACKS:
                hit = sum_in[back - 1, 0:1, :] == sens_in[place, 1:2, :]
                value = value + jnp.where(hit, moved[back - 1], 0.0)
            adj_out[place, plain(piece), :] = value
            if place:
                moved = [decay * value for value in moved]
        for step in (2, 1, 3):
            adj_copy(piece, step).start()
        adj_in[mine, plain(piece), :] = adj_out[mine, plain(piece), :]

    wait_peers(ends_in, pl.ds(0, rows), to_ends, ends_recv.at[0])
    product = ends_in[0] * adj_out[0]
    for place in range(1, CLUSTER):
        product = product + ends_in[place] * adj_out[place]
    carried = jnp.sum(product, axis=1, keepdims=True)
    for index in range(share):
        hit = filter_lane == mine * share + index
        terms = terms + jnp.where(hit, carried[index * modes : (index + 1) * modes], 0.0)
    terms = norm_of(rate_ref[...]) * terms * scale
    near_out[0] = jnp.concatenate([terms, jnp.zeros((modes, width - filters), F32)], axis=1)

    def near_copy(step):
        return pltpu.make_async_remote_copy(
            src_ref=near_out.at[0],
            dst_ref=near_in.at[near_mine],
            send_sem=send_sem.at[to_near],
            recv_sem=reduce_recv.at[0],
            device_id=near_spot(step),
            device_id_type=MESH,
        )

    def far_copy(step):
        return pltpu.make_async_remote_copy(
            src_ref=near_out.at[1],
            dst_ref=far_in.at[block],
            send_sem=send_sem.at[to_far],
            recv_sem=reduce_recv.at[1],
            device_id=far_spot(step),
            device_id_type=MESH,
        )

    def all_of(ref, count, send, recv):
        several = ref.at[pl.ds(0, count)]
        return to_peer(several, several, send, recv, 1)

    near_all = all_of(near_in, near_count - 1, to_near, reduce_recv.at[0])
    far_all = all_of(far_in, clusters - 1, to_far, reduce_recv.at[1])

    for step in range(1, near_count):
        near_copy(step).start()
    near_in[near_mine] = near_out[0]

    lax.fori_loop(0, filters, near_by, 0, unroll=16)

    near_all.wait_recv()
    near_total = near_in[0]
    for rank in range(1, near_count):
        near_total = near_total + near_in[rank]
    near_out[1] = near_total
    for step in range(1, clusters):
        far_copy(step).start()
    far_in[block] = near_total

    def finish(index):
        high_low = edges[edge_rows(index), :]
        spot = pl.ds(pl.multiple_of(lax.rem(index, share) * modes, modes), modes)
        adjoint = adj_in[index // share, spot, :]
        adj_high, adj_low = two_parts(weights[table_rows(index), :] * adjoint)
        left = jnp.concatenate([high_low, high_low[:modes]], axis=0)
        right = jnp.concatenate([adj_high, adj_high, adj_low], axis=0)
        carried = dot(left, right, ((0,), (0,)))
        grad_ref[:, group(index)] = (local[:, group(index)] + carried).astype(BF16)

    for piece in range(PIECES):
        wait_peers(adj_in, plain(piece), to_adj, adj_recv.at[piece])

        def finish_one(turn, carry, piece=piece):
            finish(turn // batch * share + piece * batch + lax.rem(turn, batch))
            return carry

        lax.fori_loop(0, CLUSTER * batch, finish_one, 0, unroll=8)

    far_all.wait_recv()
    far_total = far_in[0]
    for rank in range(1, clusters):
        far_total = far_total + far_in[rank]
    term_ref[...] = far_total[:, :filters]

    wait_sent(sens_out, to_sens)
    wait_sent(ends_out, to_ends)
    wait_sent(adj_out, to_adj)
    near_all.wait_send()
    far_all.wait_send()
    for back in BACKS:

        @pl.when(me - back * CLUSTER >= 0)
        def _(back=back):
            pltpu.make_async_remote_copy(
                src_ref=sum_out,
                dst_ref=sum_in.at[back - 1],
                send_sem=sum_send.at[back - 1],
                recv_sem=sum_recv.at[0, back - 1],
                device_id={"ctx": me - back * CLUSTER},
                device_id_type=MESH,
            ).wait_send()


def store(grad_ref, term_ref, grad_hbm, term_hbm, sems):
    copies = [
        pltpu.make_async_copy(term_ref, term_hbm, sems.at[0]),
        pltpu.make_async_copy(grad_ref, grad_hbm, sems.at[1]),
    ]
    for copy in copies:
        copy.start()
    for copy in copies:
        copy.wait()


def body(signal, cotangent, record_id, rate, residue):
    length, width = signal.shape[1:]
    filters, modes = rate.shape
    shards = lax.axis_size("ctx")
    group_width = width // filters
    rows = filters // CLUSTER * modes
    sequences = signal.shape[0] * lax.axis_size("dp")
    scale = 1.0 / math.sqrt(sequences * length * shards * group_width)
    copies = lax.axis_size("dp")
    near_count = CLUSTER * copies
    clusters = shards // CLUSTER
    hbm = pl.BlockSpec(memory_space=pltpu.HBM)
    vmem = pl.BlockSpec(memory_space=pltpu.VMEM)
    in_hbm = functools.partial(pltpu.with_memory_space_constraint, memory_space=pltpu.HBM)
    in_vmem = functools.partial(pltpu.with_memory_space_constraint, memory_space=pltpu.VMEM)
    dma = pltpu.SemaphoreType.DMA
    grad, terms = pl.pallas_call(
        functools.partial(kernel, filters, modes, shards, scale, copies),
        out_shape=(pltpu.VMEM((length, width), BF16), pltpu.VMEM((modes, filters), F32)),
        in_specs=[hbm] * 5,
        out_specs=(vmem, vmem),
        scratch_shapes=[
            pltpu.VMEM((length, width), BF16),
            pltpu.VMEM((length, width), BF16),
            pltpu.VMEM(record_id.shape, jnp.int32),
            pltpu.VMEM((modes, filters), F32),
            pltpu.VMEM((modes, filters), F32),
            pltpu.VMEM((filters * modes, group_width), F32),
            pltpu.VMEM((filters * modes, group_width), F32),
            pltpu.VMEM((length, length), F32),
            pltpu.VMEM((filters * 2 * modes, length), BF16),
            pltpu.VMEM((length, width), F32),
            pltpu.VMEM((CLUSTER, rows + 8, group_width), F32),
            pltpu.VMEM((CLUSTER, rows + 8, group_width), F32),
            pltpu.VMEM((CLUSTER, rows, group_width), F32),
            pltpu.VMEM((CLUSTER, rows, group_width), F32),
            pltpu.VMEM((rows + 8, group_width), F32),
            pltpu.VMEM((2, rows + 8, group_width), F32),
            pltpu.VMEM((CLUSTER, rows, group_width), F32),
            pltpu.VMEM((CLUSTER, rows, group_width), F32),
            pltpu.VMEM((2, modes, group_width), F32),
            pltpu.VMEM((near_count, modes, group_width), F32),
            pltpu.VMEM((clusters, modes, group_width), F32),
            dma((5,)),
            dma((2,)),
            dma((PIECES,)),
            dma((1,)),
            dma((PIECES, 2)),
            dma((PIECES,)),
            dma((2,)),
            dma((5,)),
        ],
        compiler_params=pltpu.CompilerParams(
            collective_id=0, has_side_effects=True, vmem_limit_bytes=52 << 20
        ),
    )(*(in_hbm(x) for x in (signal[0], cotangent[0], record_id, rate.T, residue.T)))
    grad, terms = pl.pallas_call(
        store,
        out_shape=(
            jax.ShapeDtypeStruct((length, width), BF16),
            jax.ShapeDtypeStruct((modes, filters), F32),
        ),
        in_specs=[vmem, vmem],
        out_specs=(hbm, hbm),
        scratch_shapes=[dma((2,))],
    )(in_vmem(grad), in_vmem(terms))
    return grad[None], terms.T


def solution(mesh):
    return jax.shard_map(
        body,
        mesh=mesh,
        in_specs=(P("dp", "ctx", None), P("dp", "ctx", None), P("dp", "ctx"), P(), P()),
        out_specs=(P("dp", "ctx", None), P()),
        check_vma=False,
    )
```

```python
import functools
import math

import jax
import jax.numpy as jnp
from jax import lax
from jax.experimental import pallas as pl
from jax.experimental.pallas import tpu as pltpu
from jax.sharding import PartitionSpec as P

CLUSTER = 4
PIECES = 4
BACKS = (1, 2)
ONE_ROUND = 64
MESH = pl.DeviceIdType.MESH
F32 = jnp.float32
BF16 = jnp.bfloat16


def two_parts(table):
    high = table.astype(BF16)
    return high, (table - high.astype(F32)).astype(BF16)


def dot(left, right, contract=((1,), (0,))):
    return lax.dot_general(left, right, (contract, ((), ())), preferred_element_type=F32)


def row_sums(table):
    return jnp.sum(table.T, axis=0, keepdims=True)


def round_of(shards, copies):
    return shards if shards * copies <= ONE_ROUND else CLUSTER


def kernel(
    filters,
    modes,
    shards,
    scale,
    copies,
    signal_hbm,
    cotangent_hbm,
    record_hbm,
    rate_hbm,
    residue_hbm,
    grad_ref,
    total_ref,
    norm_ref,
    signal_ref,
    cotangent_ref,
    record_ref,
    rate_ref,
    residue_ref,
    rates,
    weights,
    mask,
    edges,
    local,
    within,
    within_out,
    within_in,
    sens_out,
    sens_in,
    ends_out,
    ends_in,
    sum_out,
    sum_in,
    adj_out,
    adj_in,
    near_out,
    near_in,
    far_out,
    far_in,
    send_sem,
    sum_send,
    sens_recv,
    ends_recv,
    within_recv,
    sum_recv,
    adj_recv,
    reduce_recv,
    fetch_sem,
):
    length = signal_ref.shape[0]
    width = signal_ref.shape[1] // filters
    share = filters // CLUSTER
    rows = share * modes
    depth = rows // PIECES
    batch = share // PIECES
    me = lax.axis_index("ctx")
    mine = lax.rem(me, CLUSTER)
    home = me - mine
    copy_of = lax.axis_index("dp")
    round_size = round_of(shards, copies)
    near_count = round_size * copies
    rounds = shards // round_size
    block = me // round_size
    in_round = lax.rem(me, round_size)
    near_mine = copy_of * round_size + in_round
    to_sens, to_ends, to_adj, to_near, to_far, to_within = range(6)

    def near_spot(step):
        rank = lax.rem(near_mine + step, near_count)
        return {"ctx": block * round_size + lax.rem(rank, round_size), "dp": rank // round_size}

    def far_spot(step):
        return {"ctx": lax.rem(block + step, rounds) * round_size + in_round, "dp": copy_of}

    fetches = [
        pltpu.make_async_copy(source, target, fetch_sem.at[place])
        for place, (source, target) in enumerate(
            (
                (record_hbm, record_ref),
                (rate_hbm, rate_ref),
                (residue_hbm, residue_ref),
                (cotangent_hbm, cotangent_ref),
                (signal_hbm, signal_ref),
            )
        )
    ]
    for fetch in fetches:
        fetch.start()
    barrier = pltpu.get_barrier_semaphore()
    for step in range(1, near_count):
        pl.semaphore_signal(barrier, inc=1, device_id=near_spot(step), device_id_type=MESH)
    for step in range(1, rounds):
        pl.semaphore_signal(barrier, inc=1, device_id=far_spot(step), device_id_type=MESH)

    lane = lax.broadcasted_iota(jnp.int32, (modes, length), 1).astype(F32)
    filter_lane = lax.broadcasted_iota(jnp.int32, (modes, filters), 1)
    tag_row = lax.broadcasted_iota(jnp.int32, (8, width), 0)
    row = lax.broadcasted_iota(jnp.int32, (length, length), 0)
    column = lax.broadcasted_iota(jnp.int32, (length, length), 1)
    for fetch in fetches[:3]:
        fetch.wait()
    ids = jnp.broadcast_to(record_ref[...].astype(F32), (length, length))
    first = ids[:8, :1]
    last = ids[:8, length - 1 :]
    in_first = (ids[:1] == first[:1]).astype(F32)
    in_last = (ids[:1] == last[:1]).astype(F32)
    tag = jnp.where(tag_row == 0, first, last)

    def group(index):
        return pl.ds(pl.multiple_of(index * width, width), width)

    def table_rows(index):
        return pl.ds(pl.multiple_of(index * modes, modes), modes)

    def edge_rows(index):
        return pl.ds(pl.multiple_of(index * 2 * modes, 2 * modes), 2 * modes)

    def column_of(ref, index):
        return jnp.sum(jnp.where(filter_lane == index, ref[...], 0.0), axis=1, keepdims=True)

    def norm_of(rate):
        double = 2.0 * rate
        series = 1.0 - double * (1.0 / 6.0) * (1.0 - double * (1.0 / 7.0))
        for divisor in (5.0, 4.0, 3.0, 2.0):
            series = 1.0 - double * (1.0 / divisor) * series
        return jnp.sqrt(double * series)

    def tagged(piece):
        return pl.ds(0, depth + 8) if piece == 0 else pl.ds(8 + piece * depth, depth)

    def plain(piece):
        return pl.ds(piece * depth, depth)

    def to_peer(source, target, send, recv, step):
        return pltpu.make_async_remote_copy(
            src_ref=source,
            dst_ref=target,
            send_sem=send_sem.at[send],
            recv_sem=recv,
            device_id={"ctx": home + lax.rem(mine + step, CLUSTER)},
            device_id_type=MESH,
        )

    def sens_copy(piece, step):
        peer = lax.rem(mine + step, CLUSTER)
        return to_peer(
            sens_out.at[peer, tagged(piece)],
            sens_in.at[mine, tagged(piece)],
            to_sens,
            sens_recv.at[piece],
            step,
        )

    def ends_copy(piece, step):
        peer = lax.rem(mine + step, CLUSTER)
        return to_peer(
            ends_out.at[peer, plain(piece)],
            ends_in.at[mine, plain(piece)],
            to_ends,
            ends_recv.at[0],
            step,
        )

    def adj_copy(piece, step):
        peer = lax.rem(mine + step, CLUSTER)
        return to_peer(
            adj_out.at[peer, plain(piece)],
            adj_in.at[mine, plain(piece)],
            to_adj,
            adj_recv.at[piece],
            step,
        )

    def wait_peers(ref, span, send, recv):
        several = ref.at[pl.ds(0, CLUSTER - 1), span]
        to_peer(several, several, send, recv, 1).wait_recv()

    def wait_sent(ref, send):
        several = ref.at[pl.ds(0, CLUSTER - 1)]
        to_peer(several, several, send, ends_recv.at[0], 1).wait_send()

    def sum_copy(piece, back):
        return pltpu.make_async_remote_copy(
            src_ref=sum_out.at[tagged(piece)],
            dst_ref=sum_in.at[back - 1, tagged(piece)],
            send_sem=sum_send.at[back - 1],
            recv_sem=sum_recv.at[piece, back - 1],
            device_id={"ctx": me - back * CLUSTER},
            device_id_type=MESH,
        )

    def sense(index):
        rate = jnp.broadcast_to(column_of(rate_ref, index), (modes, width))
        rates[table_rows(index), :] = rate
        weights[table_rows(index), :] = norm_of(rate) * column_of(residue_ref, index)
        high, low = two_parts(jnp.exp(-rate * (lane + 1.0)) * in_first)
        both = dot(jnp.concatenate([high, low], axis=0), cotangent_ref[:, group(index)])
        spot = pl.ds(pl.multiple_of(8 + lax.rem(index, share) * modes, 8), modes)
        sens_out[index // share, spot, :] = both[:modes] + both[modes:]

    def end(index):
        rate = rates[table_rows(index), :]
        high, low = two_parts(jnp.exp(-rate * (length - 1.0 - lane)) * in_last)
        pair = jnp.concatenate([high, low], axis=0)
        edges[edge_rows(index), :] = pair
        both = dot(pair, signal_ref[:, group(index)])
        spot = pl.ds(pl.multiple_of(lax.rem(index, share) * modes, modes), modes)
        ends_out[index // share, spot, :] = both[:modes] + both[modes:]

    row_of = lax.broadcasted_iota(jnp.int32, (8, length), 0)

    def intra(index, carry):
        rate = rates[table_rows(index), :]
        products = dot(signal_ref[:, group(index)], cotangent_ref[:, group(index)], ((1,), (1,)))
        products = products * mask[...]
        parts = [products[:8]]
        for start in range(8, length, 8):
            parts.append(pltpu.roll(products[start : start + 8], length - start, 1))
        while len(parts) > 1:
            parts = [parts[i] + parts[i + 1] for i in range(0, len(parts), 2)]
        by_lag = parts[0]
        for bit in (1, 2, 4):
            moved = pltpu.roll(by_lag, length - bit, 1)
            by_lag = jnp.where((row_of & bit) != 0, moved, by_lag)
        by_lag = jnp.sum(by_lag, axis=0, keepdims=True)
        within[table_rows(index), :] = by_lag * jnp.exp(-rate * lane)
        return carry

    def near_by(index, carry):
        rate = rates[table_rows(index), :]
        weight = weights[table_rows(index), :]
        lags = jnp.sum(weight * jnp.exp(-rate * lane), axis=0, keepdims=True)
        spread = pltpu.roll(
            jnp.broadcast_to(lags, (length, length)), 0, 1, stride=1, stride_axis=0
        )
        kernel_now = (spread * mask[...]).astype(BF16)
        local[:, group(index)] = dot(kernel_now, cotangent_ref[:, group(index)])
        return carry

    for part in range(CLUSTER):
        sens_out[part, :8, :] = tag
    for back in BACKS:

        @pl.when(me + back * CLUSTER >= shards)
        def _(back=back):
            sum_in[back - 1] = jnp.full(sum_in.shape[1:], -1.0, F32)

    fetches[3].wait()
    for piece in range(PIECES):
        for step in (2, 1, 3, 0):
            base = lax.rem(mine + step, CLUSTER) * share + piece * batch
            for index in range(batch):
                sense(base + index)
        if piece == 0:
            pl.semaphore_wait(barrier, near_count + rounds - 2)
        for step in (2, 1, 3):
            sens_copy(piece, step).start()
        sens_in[mine, tagged(piece), :] = sens_out[mine, tagged(piece), :]
    mask[...] = jnp.where((ids == ids.T) & (column >= row), 1.0, 0.0)
    fetches[4].wait()
    for piece in range(PIECES):
        for step in (2, 1, 3, 0):
            base = lax.rem(mine + step, CLUSTER) * share + piece * batch
            for index in range(batch):
                end(base + index)
    for piece in range(PIECES):
        for step in (2, 1, 3):
            ends_copy(piece, step).start()
        ends_in[mine, plain(piece), :] = ends_out[mine, plain(piece), :]

    def decay_of(piece):
        start = pl.multiple_of(mine * rows + piece * depth, 8)
        return jnp.exp(-rates[pl.ds(start, depth), :] * float(length))

    lax.fori_loop(0, filters // 2, intra, 0, unroll=16)

    for piece in range(PIECES):
        wait_peers(sens_in, tagged(piece), to_sens, sens_recv.at[piece])
        decay = decay_of(piece)
        firsts = [sens_in[place, 0:1, :] for place in range(CLUSTER)]
        lasts = [sens_in[place, 1:2, :] for place in range(CLUSTER)]
        span = pl.ds(8 + piece * depth, depth)
        values = []
        value = jnp.zeros((depth, width), F32)
        for place in range(CLUSTER - 1, -1, -1):
            values.append(value)
            value = jnp.where(firsts[place] == lasts[place], decay * value, 0.0)
            value = sens_in[place, span, :] + value
            if place:
                value = jnp.where(firsts[place] == lasts[place - 1], value, 0.0)
        sum_out[span, :] = value
        if piece == 0:
            sum_out[:8, :] = sens_in[0, :8, :]
        for back in BACKS:

            @pl.when(me - back * CLUSTER >= 0)
            def _(piece=piece, back=back):
                sum_copy(piece, back).start()

        for place, value in enumerate(reversed(values)):
            adj_out[place, plain(piece), :] = value

    lax.fori_loop(filters // 2, filters, intra, 0, unroll=16)
    for part in range(CLUSTER):
        within_out[part] = row_sums(within[part * rows : (part + 1) * rows, :])
    for step in (2, 1, 3):
        peer = lax.rem(mine + step, CLUSTER)
        to_peer(
            within_out.at[peer], within_in.at[mine], to_within, within_recv.at[0], step
        ).start()
    within_in[mine] = within_out[mine]

    for piece in range(PIECES):
        for back in BACKS:

            @pl.when(me + back * CLUSTER < shards)
            def _(piece=piece, back=back):
                sum_copy(piece, back).wait_recv()

        decay = decay_of(piece)
        span = pl.ds(8 + piece * depth, depth)
        fourth = decay * decay
        fourth = fourth * fourth
        moved = [sum_in[0, span, :], fourth * sum_in[1, span, :]]
        for place in range(CLUSTER - 1, -1, -1):
            value = adj_out[place, plain(piece), :]
            for back in BACKS:
                hit = sum_in[back - 1, 0:1, :] == sens_in[place, 1:2, :]
                value = value + jnp.where(hit, moved[back - 1], 0.0)
            adj_out[place, plain(piece), :] = value
            if place:
                moved = [decay * value for value in moved]
        for step in (2, 1, 3):
            adj_copy(piece, step).start()
        adj_in[mine, plain(piece), :] = adj_out[mine, plain(piece), :]

    wait_peers(ends_in, pl.ds(0, rows), to_ends, ends_recv.at[0])
    product = ends_in[0] * adj_out[0]
    for place in range(1, CLUSTER):
        product = product + ends_in[place] * adj_out[place]
    wait_peers(within_in, pl.ds(0, 1), to_within, within_recv.at[0])
    terms = row_sums(product)
    for place in range(CLUSTER):
        terms = terms + within_in[place]
    near_out[0] = terms

    def near_copy(step):
        return pltpu.make_async_remote_copy(
            src_ref=near_out.at[0],
            dst_ref=near_in.at[near_mine],
            send_sem=send_sem.at[to_near],
            recv_sem=reduce_recv.at[0],
            device_id=near_spot(step),
            device_id_type=MESH,
        )

    def far_copy(step):
        return pltpu.make_async_remote_copy(
            src_ref=far_out,
            dst_ref=far_in.at[block],
            send_sem=send_sem.at[to_far],
            recv_sem=reduce_recv.at[1],
            device_id=far_spot(step),
            device_id_type=MESH,
        )

    def all_of(ref, count, send, recv):
        several = ref.at[pl.ds(0, count)]
        return to_peer(several, several, send, recv, 1)

    near_all = all_of(near_in, near_count - 1, to_near, reduce_recv.at[0])
    far_all = all_of(far_in, rounds - 1, to_far, reduce_recv.at[1]) if rounds > 1 else None

    for step in range(1, near_count):
        near_copy(step).start()
    near_in[near_mine] = near_out[0]
    norm_ref[...] = norm_of(rate_ref[...]) * scale

    lax.fori_loop(0, filters, near_by, 0, unroll=16)

    def gather_near():
        near_all.wait_recv()
        for part in range(CLUSTER):
            total = near_in[part]
            for rank in range(part + CLUSTER, near_count, CLUSTER):
                total = total + near_in[rank]
            total_ref[part : part + 1, :] = total

    if rounds > 1:
        gather_near()
        far_out[...] = total_ref[...]
        for step in range(1, rounds):
            far_copy(step).start()
        far_in[block] = far_out[...]

    def finish(index):
        high_low = edges[edge_rows(index), :]
        spot = pl.ds(pl.multiple_of(lax.rem(index, share) * modes, modes), modes)
        adjoint = adj_in[index // share, spot, :]
        adj_high, adj_low = two_parts(weights[table_rows(index), :] * adjoint)
        left = jnp.concatenate([high_low, high_low[:modes]], axis=0)
        right = jnp.concatenate([adj_high, adj_high, adj_low], axis=0)
        carried = dot(left, right, ((0,), (0,)))
        grad_ref[:, group(index)] = (local[:, group(index)] + carried).astype(BF16)

    for piece in range(PIECES):
        wait_peers(adj_in, plain(piece), to_adj, adj_recv.at[piece])

        def finish_one(turn, carry, piece=piece):
            finish(turn // batch * share + piece * batch + lax.rem(turn, batch))
            return carry

        lax.fori_loop(0, CLUSTER * batch, finish_one, 0, unroll=8)

    if rounds > 1:
        far_all.wait_recv()
        far_total = far_in[0]
        for rank in range(1, rounds):
            far_total = far_total + far_in[rank]
        total_ref[...] = far_total
    else:
        gather_near()

    wait_sent(sens_out, to_sens)
    wait_sent(ends_out, to_ends)
    wait_sent(adj_out, to_adj)
    wait_sent(within_out, to_within)
    near_all.wait_send()
    if rounds > 1:
        far_all.wait_send()
    for back in BACKS:

        @pl.when(me - back * CLUSTER >= 0)
        def _(back=back):
            pltpu.make_async_remote_copy(
                src_ref=sum_out,
                dst_ref=sum_in.at[back - 1],
                send_sem=sum_send.at[back - 1],
                recv_sem=sum_recv.at[0, back - 1],
                device_id={"ctx": me - back * CLUSTER},
                device_id_type=MESH,
            ).wait_send()


def store(grad_ref, total_ref, norm_ref, grad_hbm, term_hbm, term_ref, sems):
    write_grad = pltpu.make_async_copy(grad_ref, grad_hbm, sems.at[0])
    write_grad.start()
    modes, filters = norm_ref.shape
    parts, rows = total_ref.shape
    share = filters // parts
    row = lax.broadcasted_iota(jnp.int32, (rows, filters), 0)
    column = lax.broadcasted_iota(jnp.int32, (rows, filters), 1)
    lane = lax.broadcasted_iota(jnp.int32, (modes, rows), 1)
    mode = lax.broadcasted_iota(jnp.int32, (modes, rows), 0)
    own = (lane & (modes - 1)) == mode
    total = jnp.zeros((3 * modes, filters), F32)
    for part in range(parts):
        spread = jnp.where(own, total_ref[part : part + 1, :], 0.0)
        high, rest = spread.astype(BF16), spread - spread.astype(BF16).astype(F32)
        middle, low = two_parts(rest)
        start = (column - part * share) * modes
        pick = jnp.where((row >= start) & (row < start + modes), 1.0, 0.0).astype(BF16)
        total = total + dot(jnp.concatenate([high, middle, low], axis=0), pick)
    total = total[:modes] + (total[modes : 2 * modes] + total[2 * modes :])
    term_ref[...] = norm_ref[...] * total
    write_term = pltpu.make_async_copy(term_ref, term_hbm, sems.at[1])
    write_term.start()
    write_term.wait()
    write_grad.wait()


def body(signal, cotangent, record_id, rate, residue):
    length, width = signal.shape[1:]
    filters, modes = rate.shape
    shards = lax.axis_size("ctx")
    group_width = width // filters
    rows = filters // CLUSTER * modes
    sequences = signal.shape[0] * lax.axis_size("dp")
    scale = 1.0 / math.sqrt(sequences * length * shards * group_width)
    copies = lax.axis_size("dp")
    near_count = round_of(shards, copies) * copies
    rounds = shards // round_of(shards, copies)
    hbm = pl.BlockSpec(memory_space=pltpu.HBM)
    vmem = pl.BlockSpec(memory_space=pltpu.VMEM)
    in_hbm = functools.partial(pltpu.with_memory_space_constraint, memory_space=pltpu.HBM)
    in_vmem = functools.partial(pltpu.with_memory_space_constraint, memory_space=pltpu.VMEM)
    dma = pltpu.SemaphoreType.DMA
    grad, total, norm = pl.pallas_call(
        functools.partial(kernel, filters, modes, shards, scale, copies),
        out_shape=(
            pltpu.VMEM((length, width), BF16),
            pltpu.VMEM((CLUSTER, rows), F32),
            pltpu.VMEM((modes, filters), F32),
        ),
        in_specs=[hbm] * 5,
        out_specs=(vmem, vmem, vmem),
        scratch_shapes=[
            pltpu.VMEM((length, width), BF16),
            pltpu.VMEM((length, width), BF16),
            pltpu.VMEM(record_id.shape, jnp.int32),
            pltpu.VMEM((modes, filters), F32),
            pltpu.VMEM((modes, filters), F32),
            pltpu.VMEM((filters * modes, group_width), F32),
            pltpu.VMEM((filters * modes, group_width), F32),
            pltpu.VMEM((length, length), F32),
            pltpu.VMEM((filters * 2 * modes, length), BF16),
            pltpu.VMEM((length, width), F32),
            pltpu.VMEM((filters * modes, length), F32),
            pltpu.VMEM((CLUSTER, 1, rows), F32),
            pltpu.VMEM((CLUSTER, 1, rows), F32),
            pltpu.VMEM((CLUSTER, rows + 8, group_width), F32),
            pltpu.VMEM((CLUSTER, rows + 8, group_width), F32),
            pltpu.VMEM((CLUSTER, rows, group_width), F32),
            pltpu.VMEM((CLUSTER, rows, group_width), F32),
            pltpu.VMEM((rows + 8, group_width), F32),
            pltpu.VMEM((2, rows + 8, group_width), F32),
            pltpu.VMEM((CLUSTER, rows, group_width), F32),
            pltpu.VMEM((CLUSTER, rows, group_width), F32),
            pltpu.VMEM((1, 1, rows), F32),
            pltpu.VMEM((near_count, 1, rows), F32),
            pltpu.VMEM((CLUSTER, rows), F32),
            pltpu.VMEM((rounds, CLUSTER, rows), F32),
            dma((6,)),
            dma((2,)),
            dma((PIECES,)),
            dma((1,)),
            dma((1,)),
            dma((PIECES, 2)),
            dma((PIECES,)),
            dma((2,)),
            dma((5,)),
        ],
        compiler_params=pltpu.CompilerParams(
            collective_id=0, has_side_effects=True, vmem_limit_bytes=52 << 20
        ),
    )(*(in_hbm(x) for x in (signal[0], cotangent[0], record_id, rate.T, residue.T)))
    grad, terms = pl.pallas_call(
        store,
        out_shape=(
            jax.ShapeDtypeStruct((length, width), BF16),
            jax.ShapeDtypeStruct((modes, filters), F32),
        ),
        in_specs=[vmem, vmem, vmem],
        out_specs=(hbm, hbm),
        scratch_shapes=[pltpu.VMEM((modes, filters), F32), dma((2,))],
    )(in_vmem(grad), in_vmem(total), in_vmem(norm))
    return grad[None], terms.T


def solution(mesh):
    return jax.shard_map(
        body,
        mesh=mesh,
        in_specs=(P("dp", "ctx", None), P("dp", "ctx", None), P("dp", "ctx"), P(), P()),
        out_specs=(P("dp", "ctx", None), P()),
        check_vma=False,
    )
```

```python
import functools
import math

import jax
import jax.numpy as jnp
from jax import lax
from jax.experimental import pallas as pl
from jax.experimental.pallas import tpu as pltpu
from jax.sharding import PartitionSpec as P

CLUSTER = 4
PIECES = 4
BACKS = (1, 2)
ONE_ROUND = 64
MESH = pl.DeviceIdType.MESH
F32 = jnp.float32
BF16 = jnp.bfloat16


def two_parts(table):
    high = table.astype(BF16)
    return high, (table - high.astype(F32)).astype(BF16)


def dot(left, right, contract=((1,), (0,))):
    return lax.dot_general(left, right, (contract, ((), ())), preferred_element_type=F32)


def row_sums(table):
    return jnp.sum(table.T, axis=0, keepdims=True)


def round_of(shards, copies):
    return shards if shards * copies <= ONE_ROUND else CLUSTER


def kernel(
    filters,
    modes,
    shards,
    scale,
    copies,
    signal_hbm,
    cotangent_hbm,
    record_hbm,
    rate_hbm,
    residue_hbm,
    grad_ref,
    total_ref,
    norm_ref,
    signal_ref,
    cotangent_ref,
    record_ref,
    rate_ref,
    residue_ref,
    rates,
    weights,
    mask,
    edges,
    starts,
    local,
    within,
    within_out,
    within_in,
    sens_out,
    sens_in,
    ends_out,
    ends_in,
    sum_out,
    sum_in,
    adj_out,
    adj_in,
    near_out,
    near_in,
    far_out,
    far_in,
    send_sem,
    sum_send,
    sens_recv,
    ends_recv,
    within_recv,
    sum_recv,
    adj_recv,
    reduce_recv,
    fetch_sem,
    entered,
):
    length = signal_ref.shape[0]
    width = signal_ref.shape[1] // filters
    share = filters // CLUSTER
    rows = share * modes
    depth = rows // PIECES
    batch = share // PIECES
    me = lax.axis_index("ctx")
    mine = lax.rem(me, CLUSTER)
    home = me - mine
    copy_of = lax.axis_index("dp")
    planes = shards // CLUSTER
    plane = me // CLUSTER
    round_size = round_of(shards, copies)
    near_count = round_size * copies
    rounds = shards // round_size
    block = me // round_size
    in_round = lax.rem(me, round_size)
    near_mine = copy_of * round_size + in_round
    bits = round_size.bit_length() - 1
    others = [copy_of] + [lax.rem(copy_of + step, copies) for step in range(1, copies)]
    far_first = sorted(range(1, near_count), key=lambda step: -step.bit_count())
    to_sens, to_ends, to_adj, to_near, to_far, to_within = range(6)

    turns = [(1 << bit) * (1 - 2 * lax.rem(me // (1 << bit), 2)) for bit in range(bits)]

    def near_spot(step):
        flips, other = step % round_size, step // round_size
        spot = me
        for bit in range(bits):
            if flips >> bit & 1:
                spot = spot + turns[bit]
        return {"ctx": spot, "dp": others[other]}

    def far_spot(step):
        return {"ctx": lax.rem(block + step, rounds) * round_size + in_round, "dp": copy_of}

    fetches = [
        pltpu.make_async_copy(source, target, fetch_sem.at[place])
        for place, (source, target) in enumerate(
            (
                (record_hbm, record_ref),
                (rate_hbm, rate_ref),
                (residue_hbm, residue_ref),
                (cotangent_hbm, cotangent_ref),
                (signal_hbm, signal_ref),
            )
        )
    ]
    for fetch in fetches:
        fetch.start()
    barrier = pltpu.get_barrier_semaphore()
    plane_count = CLUSTER * copies
    for step in range(1, plane_count):
        spot = near_spot(step // CLUSTER * round_size + step % CLUSTER)
        pl.semaphore_signal(barrier, inc=1, device_id=spot, device_id_type=MESH)

    def tell_higher(semaphore):
        for step in range(1, planes):

            @pl.when(plane + step < planes)
            def _(step=step):
                spot = {"ctx": me + step * CLUSTER}
                pl.semaphore_signal(semaphore, inc=1, device_id=spot, device_id_type=MESH)

    def tell_lower(semaphore):
        for step in range(1, planes):

            @pl.when(plane - step >= 0)
            def _(step=step):
                spot = {"ctx": me - step * CLUSTER}
                pl.semaphore_signal(semaphore, inc=1, device_id=spot, device_id_type=MESH)

    tell_higher(barrier)

    def wait_some(semaphore, count):
        @pl.when(count > 0)
        def _():
            pl.semaphore_wait(semaphore, count)

    lane = lax.broadcasted_iota(jnp.int32, (modes, length), 1).astype(F32)
    filter_lane = lax.broadcasted_iota(jnp.int32, (modes, filters), 1)
    tag_row = lax.broadcasted_iota(jnp.int32, (8, width), 0)
    row = lax.broadcasted_iota(jnp.int32, (length, length), 0)
    column = lax.broadcasted_iota(jnp.int32, (length, length), 1)
    for fetch in fetches[:3]:
        fetch.wait()
    ids = jnp.broadcast_to(record_ref[...].astype(F32), (length, length))
    first = ids[:8, :1]
    last = ids[:8, length - 1 :]
    in_first = (ids[:1] == first[:1]).astype(F32)
    in_last = (ids[:1] == last[:1]).astype(F32)
    tag = jnp.where(tag_row == 0, first, last)

    def group(index):
        return pl.ds(pl.multiple_of(index * width, width), width)

    def table_rows(index):
        return pl.ds(pl.multiple_of(index * modes, modes), modes)

    def edge_rows(index):
        return pl.ds(pl.multiple_of(index * 2 * modes, 2 * modes), 2 * modes)

    def column_of(ref, index):
        return jnp.sum(jnp.where(filter_lane == index, ref[...], 0.0), axis=1, keepdims=True)

    def norm_of(rate):
        double = 2.0 * rate
        series = 1.0 - double * (1.0 / 6.0) * (1.0 - double * (1.0 / 7.0))
        for divisor in (5.0, 4.0, 3.0, 2.0):
            series = 1.0 - double * (1.0 / divisor) * series
        return jnp.sqrt(double * series)

    def tagged(piece):
        return pl.ds(0, depth + 8) if piece == 0 else pl.ds(8 + piece * depth, depth)

    def plain(piece):
        return pl.ds(piece * depth, depth)

    def to_peer(source, target, send, recv, step):
        return pltpu.make_async_remote_copy(
            src_ref=source,
            dst_ref=target,
            send_sem=send_sem.at[send],
            recv_sem=recv,
            device_id={"ctx": home + lax.rem(mine + step, CLUSTER)},
            device_id_type=MESH,
        )

    def sens_copy(piece, step):
        peer = lax.rem(mine + step, CLUSTER)
        return to_peer(
            sens_out.at[peer, tagged(piece)],
            sens_in.at[mine, tagged(piece)],
            to_sens,
            sens_recv.at[piece],
            step,
        )

    def ends_copy(piece, step):
        peer = lax.rem(mine + step, CLUSTER)
        return to_peer(
            ends_out.at[peer, plain(piece)],
            ends_in.at[mine, plain(piece)],
            to_ends,
            ends_recv.at[0],
            step,
        )

    def adj_copy(piece, step):
        peer = lax.rem(mine + step, CLUSTER)
        return to_peer(
            adj_out.at[peer, plain(piece)],
            adj_in.at[mine, plain(piece)],
            to_adj,
            adj_recv.at[piece],
            step,
        )

    def wait_peers(ref, span, send, recv):
        several = ref.at[pl.ds(0, CLUSTER - 1), span]
        to_peer(several, several, send, recv, 1).wait_recv()

    def wait_sent(ref, send):
        several = ref.at[pl.ds(0, CLUSTER - 1)]
        to_peer(several, several, send, ends_recv.at[0], 1).wait_send()

    def sum_copy(piece, back):
        return pltpu.make_async_remote_copy(
            src_ref=sum_out.at[tagged(piece)],
            dst_ref=sum_in.at[back - 1, tagged(piece)],
            send_sem=sum_send.at[back - 1],
            recv_sem=sum_recv.at[piece, back - 1],
            device_id={"ctx": me - back * CLUSTER},
            device_id_type=MESH,
        )

    def prepare(index):
        rate = jnp.broadcast_to(column_of(rate_ref, index), (modes, width))
        rates[table_rows(index), :] = rate
        high, low = two_parts(jnp.exp(-rate * (lane + 1.0)) * in_first)
        starts[edge_rows(index), :] = jnp.concatenate([high, low], axis=0)

    def sense(index):
        both = dot(starts[edge_rows(index), :], cotangent_ref[:, group(index)])
        spot = pl.ds(pl.multiple_of(8 + lax.rem(index, share) * modes, 8), modes)
        sens_out[index // share, spot, :] = both[:modes] + both[modes:]

    def weigh(index, carry):
        norm = norm_of(rates[table_rows(index), :])
        weights[table_rows(index), :] = norm * column_of(residue_ref, index)
        return carry

    def end(index):
        rate = rates[table_rows(index), :]
        high, low = two_parts(jnp.exp(-rate * (length - 1.0 - lane)) * in_last)
        pair = jnp.concatenate([high, low], axis=0)
        edges[edge_rows(index), :] = pair
        both = dot(pair, signal_ref[:, group(index)])
        spot = pl.ds(pl.multiple_of(lax.rem(index, share) * modes, modes), modes)
        ends_out[index // share, spot, :] = both[:modes] + both[modes:]

    row_of = lax.broadcasted_iota(jnp.int32, (8, length), 0)

    def intra(index, carry):
        rate = rates[table_rows(index), :]
        products = dot(signal_ref[:, group(index)], cotangent_ref[:, group(index)], ((1,), (1,)))
        products = products * mask[...]
        parts = [products[:8]]
        for start in range(8, length, 8):
            parts.append(pltpu.roll(products[start : start + 8], length - start, 1))
        while len(parts) > 1:
            parts = [parts[i] + parts[i + 1] for i in range(0, len(parts), 2)]
        by_lag = parts[0]
        for bit in (1, 2, 4):
            moved = pltpu.roll(by_lag, length - bit, 1)
            by_lag = jnp.where((row_of & bit) != 0, moved, by_lag)
        by_lag = jnp.sum(by_lag, axis=0, keepdims=True)
        within[table_rows(index), :] = by_lag * jnp.exp(-rate * lane)
        return carry

    def near_by(index, carry):
        rate = rates[table_rows(index), :]
        weight = weights[table_rows(index), :]
        lags = jnp.sum(weight * jnp.exp(-rate * lane), axis=0, keepdims=True)
        spread = pltpu.roll(
            jnp.broadcast_to(lags, (length, length)), 0, 1, stride=1, stride_axis=0
        )
        kernel_now = (spread * mask[...]).astype(BF16)
        local[:, group(index)] = dot(kernel_now, cotangent_ref[:, group(index)])
        return carry

    for part in range(CLUSTER):
        sens_out[part, :8, :] = tag
    for back in BACKS:

        @pl.when(me + back * CLUSTER >= shards)
        def _(back=back):
            sum_in[back - 1] = jnp.full(sum_in.shape[1:], -1.0, F32)

    for index in range(filters):
        prepare(index)
    fetches[3].wait()
    for piece in range(PIECES):
        for step in (2, 1, 3, 0):
            base = lax.rem(mine + step, CLUSTER) * share + piece * batch
            for index in range(batch):
                sense(base + index)
        if piece == 0:
            pl.semaphore_wait(barrier, plane_count - 1 + plane)
            tell_lower(entered.at[0])
        for step in (2, 1, 3):
            sens_copy(piece, step).start()
        sens_in[mine, tagged(piece), :] = sens_out[mine, tagged(piece), :]
    mask[...] = jnp.where((ids == ids.T) & (column >= row), 1.0, 0.0)
    fetches[4].wait()
    for piece in range(PIECES):
        for step in (2, 1, 3, 0):
            base = lax.rem(mine + step, CLUSTER) * share + piece * batch
            for index in range(batch):
                end(base + index)
    for piece in range(PIECES):
        for step in (2, 1, 3):
            ends_copy(piece, step).start()
        ends_in[mine, plain(piece), :] = ends_out[mine, plain(piece), :]

    def decay_of(piece):
        start = pl.multiple_of(mine * rows + piece * depth, 8)
        return jnp.exp(-rates[pl.ds(start, depth), :] * float(length))

    lax.fori_loop(0, filters // 2, intra, 0, unroll=16)
    lax.fori_loop(0, filters, weigh, 0, unroll=16)

    for piece in range(PIECES):
        if piece == 2:
            lax.fori_loop(filters // 2, filters, intra, 0, unroll=16)
            for part in range(CLUSTER):
                within_out[part] = row_sums(within[part * rows : (part + 1) * rows, :])
            for step in (2, 1, 3):
                peer = lax.rem(mine + step, CLUSTER)
                to_peer(
                    within_out.at[peer], within_in.at[mine], to_within, within_recv.at[0], step
                ).start()
            within_in[mine] = within_out[mine]
        wait_peers(sens_in, tagged(piece), to_sens, sens_recv.at[piece])
        decay = decay_of(piece)
        firsts = [sens_in[place, 0:1, :] for place in range(CLUSTER)]
        lasts = [sens_in[place, 1:2, :] for place in range(CLUSTER)]
        span = pl.ds(8 + piece * depth, depth)
        values = []
        value = jnp.zeros((depth, width), F32)
        for place in range(CLUSTER - 1, -1, -1):
            values.append(value)
            value = jnp.where(firsts[place] == lasts[place], decay * value, 0.0)
            value = sens_in[place, span, :] + value
            if place:
                value = jnp.where(firsts[place] == lasts[place - 1], value, 0.0)
        sum_out[span, :] = value
        if piece == 0:
            sum_out[:8, :] = sens_in[0, :8, :]
        for back in BACKS:

            @pl.when(me - back * CLUSTER >= 0)
            def _(piece=piece, back=back):
                sum_copy(piece, back).start()

        for place, value in enumerate(reversed(values)):
            adj_out[place, plain(piece), :] = value

    wait_some(entered.at[0], planes - 1 - plane)
    tell_higher(entered.at[1])

    for piece in range(PIECES):
        for back in BACKS:

            @pl.when(me + back * CLUSTER < shards)
            def _(piece=piece, back=back):
                sum_copy(piece, back).wait_recv()

        decay = decay_of(piece)
        span = pl.ds(8 + piece * depth, depth)
        fourth = decay * decay
        fourth = fourth * fourth
        moved = [sum_in[0, span, :], fourth * sum_in[1, span, :]]
        for place in range(CLUSTER - 1, -1, -1):
            value = adj_out[place, plain(piece), :]
            for back in BACKS:
                hit = sum_in[back - 1, 0:1, :] == sens_in[place, 1:2, :]
                value = value + jnp.where(hit, moved[back - 1], 0.0)
            adj_out[place, plain(piece), :] = value
            if place:
                moved = [decay * value for value in moved]
        for step in (2, 1, 3):
            adj_copy(piece, step).start()
        adj_in[mine, plain(piece), :] = adj_out[mine, plain(piece), :]

    wait_peers(ends_in, pl.ds(0, rows), to_ends, ends_recv.at[0])
    product = ends_in[0] * adj_out[0]
    for place in range(1, CLUSTER):
        product = product + ends_in[place] * adj_out[place]
    wait_peers(within_in, pl.ds(0, 1), to_within, within_recv.at[0])
    terms = row_sums(product)
    for place in range(CLUSTER):
        terms = terms + within_in[place]
    near_out[0] = terms

    def near_copy(step):
        return pltpu.make_async_remote_copy(
            src_ref=near_out.at[0],
            dst_ref=near_in.at[near_mine],
            send_sem=send_sem.at[to_near],
            recv_sem=reduce_recv.at[0],
            device_id=near_spot(step),
            device_id_type=MESH,
        )

    def far_copy(step):
        return pltpu.make_async_remote_copy(
            src_ref=far_out,
            dst_ref=far_in.at[block],
            send_sem=send_sem.at[to_far],
            recv_sem=reduce_recv.at[1],
            device_id=far_spot(step),
            device_id_type=MESH,
        )

    def all_of(ref, count, send, recv):
        several = ref.at[pl.ds(0, count)]
        return to_peer(several, several, send, recv, 1)

    near_all = all_of(near_in, near_count - 1, to_near, reduce_recv.at[0])
    far_all = all_of(far_in, rounds - 1, to_far, reduce_recv.at[1]) if rounds > 1 else None

    wait_some(entered.at[1], plane)
    for step in far_first:
        near_copy(step).start()
    near_in[near_mine] = near_out[0]
    norm_ref[...] = norm_of(rate_ref[...]) * scale

    lax.fori_loop(0, filters, near_by, 0, unroll=16)

    def gather_near():
        near_all.wait_recv()
        for part in range(CLUSTER):
            total = near_in[part]
            for rank in range(part + CLUSTER, near_count, CLUSTER):
                total = total + near_in[rank]
            total_ref[part : part + 1, :] = total

    if rounds > 1:
        gather_near()
        far_out[...] = total_ref[...]
        for step in range(1, rounds):
            far_copy(step).start()
        far_in[block] = far_out[...]

    def finish(index):
        high_low = edges[edge_rows(index), :]
        spot = pl.ds(pl.multiple_of(lax.rem(index, share) * modes, modes), modes)
        adjoint = adj_in[index // share, spot, :]
        adj_high, adj_low = two_parts(weights[table_rows(index), :] * adjoint)
        left = jnp.concatenate([high_low, high_low[:modes]], axis=0)
        right = jnp.concatenate([adj_high, adj_high, adj_low], axis=0)
        carried = dot(left, right, ((0,), (0,)))
        grad_ref[:, group(index)] = (local[:, group(index)] + carried).astype(BF16)

    for piece in range(PIECES):
        wait_peers(adj_in, plain(piece), to_adj, adj_recv.at[piece])

        def finish_one(turn, carry, piece=piece):
            finish(turn // batch * share + piece * batch + lax.rem(turn, batch))
            return carry

        lax.fori_loop(0, CLUSTER * batch, finish_one, 0, unroll=8)

    if rounds > 1:
        far_all.wait_recv()
        far_total = far_in[0]
        for rank in range(1, rounds):
            far_total = far_total + far_in[rank]
        total_ref[...] = far_total
    else:
        gather_near()

    wait_sent(sens_out, to_sens)
    wait_sent(ends_out, to_ends)
    wait_sent(adj_out, to_adj)
    wait_sent(within_out, to_within)
    near_all.wait_send()
    if rounds > 1:
        far_all.wait_send()
    for back in BACKS:

        @pl.when(me - back * CLUSTER >= 0)
        def _(back=back):
            pltpu.make_async_remote_copy(
                src_ref=sum_out,
                dst_ref=sum_in.at[back - 1],
                send_sem=sum_send.at[back - 1],
                recv_sem=sum_recv.at[0, back - 1],
                device_id={"ctx": me - back * CLUSTER},
                device_id_type=MESH,
            ).wait_send()


def store(grad_ref, total_ref, norm_ref, grad_hbm, term_hbm, term_ref, sems):
    write_grad = pltpu.make_async_copy(grad_ref, grad_hbm, sems.at[0])
    write_grad.start()
    modes, filters = norm_ref.shape
    parts, rows = total_ref.shape
    share = filters // parts
    row = lax.broadcasted_iota(jnp.int32, (rows, filters), 0)
    column = lax.broadcasted_iota(jnp.int32, (rows, filters), 1)
    lane = lax.broadcasted_iota(jnp.int32, (modes, rows), 1)
    mode = lax.broadcasted_iota(jnp.int32, (modes, rows), 0)
    own = (lane & (modes - 1)) == mode
    total = jnp.zeros((3 * modes, filters), F32)
    for part in range(parts):
        spread = jnp.where(own, total_ref[part : part + 1, :], 0.0)
        high, rest = spread.astype(BF16), spread - spread.astype(BF16).astype(F32)
        middle, low = two_parts(rest)
        start = (column - part * share) * modes
        pick = jnp.where((row >= start) & (row < start + modes), 1.0, 0.0).astype(BF16)
        total = total + dot(jnp.concatenate([high, middle, low], axis=0), pick)
    total = total[:modes] + (total[modes : 2 * modes] + total[2 * modes :])
    term_ref[...] = norm_ref[...] * total
    write_term = pltpu.make_async_copy(term_ref, term_hbm, sems.at[1])
    write_term.start()
    write_term.wait()
    write_grad.wait()


def body(signal, cotangent, record_id, rate, residue):
    length, width = signal.shape[1:]
    filters, modes = rate.shape
    shards = lax.axis_size("ctx")
    group_width = width // filters
    rows = filters // CLUSTER * modes
    sequences = signal.shape[0] * lax.axis_size("dp")
    scale = 1.0 / math.sqrt(sequences * length * shards * group_width)
    copies = lax.axis_size("dp")
    near_count = round_of(shards, copies) * copies
    rounds = shards // round_of(shards, copies)
    hbm = pl.BlockSpec(memory_space=pltpu.HBM)
    vmem = pl.BlockSpec(memory_space=pltpu.VMEM)
    in_hbm = functools.partial(pltpu.with_memory_space_constraint, memory_space=pltpu.HBM)
    in_vmem = functools.partial(pltpu.with_memory_space_constraint, memory_space=pltpu.VMEM)
    dma = pltpu.SemaphoreType.DMA
    grad, total, norm = pl.pallas_call(
        functools.partial(kernel, filters, modes, shards, scale, copies),
        out_shape=(
            pltpu.VMEM((length, width), BF16),
            pltpu.VMEM((CLUSTER, rows), F32),
            pltpu.VMEM((modes, filters), F32),
        ),
        in_specs=[hbm] * 5,
        out_specs=(vmem, vmem, vmem),
        scratch_shapes=[
            pltpu.VMEM((length, width), BF16),
            pltpu.VMEM((length, width), BF16),
            pltpu.VMEM(record_id.shape, jnp.int32),
            pltpu.VMEM((modes, filters), F32),
            pltpu.VMEM((modes, filters), F32),
            pltpu.VMEM((filters * modes, group_width), F32),
            pltpu.VMEM((filters * modes, group_width), F32),
            pltpu.VMEM((length, length), F32),
            pltpu.VMEM((filters * 2 * modes, length), BF16),
            pltpu.VMEM((filters * 2 * modes, length), BF16),
            pltpu.VMEM((length, width), F32),
            pltpu.VMEM((filters * modes, length), F32),
            pltpu.VMEM((CLUSTER, 1, rows), F32),
            pltpu.VMEM((CLUSTER, 1, rows), F32),
            pltpu.VMEM((CLUSTER, rows + 8, group_width), F32),
            pltpu.VMEM((CLUSTER, rows + 8, group_width), F32),
            pltpu.VMEM((CLUSTER, rows, group_width), F32),
            pltpu.VMEM((CLUSTER, rows, group_width), F32),
            pltpu.VMEM((rows + 8, group_width), F32),
            pltpu.VMEM((2, rows + 8, group_width), F32),
            pltpu.VMEM((CLUSTER, rows, group_width), F32),
            pltpu.VMEM((CLUSTER, rows, group_width), F32),
            pltpu.VMEM((1, 1, rows), F32),
            pltpu.VMEM((near_count, 1, rows), F32),
            pltpu.VMEM((CLUSTER, rows), F32),
            pltpu.VMEM((rounds, CLUSTER, rows), F32),
            dma((6,)),
            dma((2,)),
            dma((PIECES,)),
            dma((1,)),
            dma((1,)),
            dma((PIECES, 2)),
            dma((PIECES,)),
            dma((2,)),
            dma((5,)),
            pltpu.SemaphoreType.REGULAR((2,)),
        ],
        compiler_params=pltpu.CompilerParams(
            collective_id=0, has_side_effects=True, vmem_limit_bytes=52 << 20
        ),
    )(*(in_hbm(x) for x in (signal[0], cotangent[0], record_id, rate.T, residue.T)))
    grad, terms = pl.pallas_call(
        store,
        out_shape=(
            jax.ShapeDtypeStruct((length, width), BF16),
            jax.ShapeDtypeStruct((modes, filters), F32),
        ),
        in_specs=[vmem, vmem, vmem],
        out_specs=(hbm, hbm),
        scratch_shapes=[pltpu.VMEM((modes, filters), F32), dma((2,))],
    )(in_vmem(grad), in_vmem(total), in_vmem(norm))
    return grad[None], terms.T


def solution(mesh):
    return jax.shard_map(
        body,
        mesh=mesh,
        in_specs=(P("dp", "ctx", None), P("dp", "ctx", None), P("dp", "ctx"), P(), P()),
        out_specs=(P("dp", "ctx", None), P()),
        check_vma=False,
    )
```

```python
import functools
import math

import jax
import jax.numpy as jnp
from jax import lax
from jax.experimental import pallas as pl
from jax.experimental.pallas import tpu as pltpu
from jax.sharding import PartitionSpec as P

CLUSTER = 4
PIECES = 4
BACKS = (1, 2)
ONE_ROUND = 64
MESH = pl.DeviceIdType.MESH
F32 = jnp.float32
BF16 = jnp.bfloat16


def two_parts(table):
    high = table.astype(BF16)
    return high, (table - high.astype(F32)).astype(BF16)


def dot(left, right, contract=((1,), (0,))):
    return lax.dot_general(left, right, (contract, ((), ())), preferred_element_type=F32)


def row_sums(table):
    return jnp.sum(table.T, axis=0, keepdims=True)


def round_of(shards, copies):
    return shards if shards * copies <= ONE_ROUND else CLUSTER


def kernel(
    filters,
    modes,
    shards,
    scale,
    copies,
    signal_hbm,
    cotangent_hbm,
    record_hbm,
    rate_hbm,
    residue_hbm,
    grad_ref,
    total_ref,
    norm_ref,
    signal_ref,
    cotangent_ref,
    record_ref,
    rate_ref,
    residue_ref,
    rates,
    weights,
    mask,
    edges,
    starts,
    local,
    within,
    within_out,
    within_in,
    sens_out,
    sens_in,
    ends_out,
    ends_in,
    sum_out,
    sum_in,
    adj_out,
    adj_in,
    near_out,
    near_in,
    far_out,
    far_in,
    send_sem,
    sum_send,
    sens_recv,
    ends_recv,
    within_recv,
    sum_recv,
    adj_recv,
    reduce_recv,
    fetch_sem,
    entered,
):
    length = signal_ref.shape[0]
    width = signal_ref.shape[1] // filters
    share = filters // CLUSTER
    rows = share * modes
    depth = rows // PIECES
    batch = share // PIECES
    me = lax.axis_index("ctx")
    mine = lax.rem(me, CLUSTER)
    home = me - mine
    copy_of = lax.axis_index("dp")
    planes = shards // CLUSTER
    plane = me // CLUSTER
    round_size = round_of(shards, copies)
    near_count = round_size * copies
    rounds = shards // round_size
    block = me // round_size
    in_round = lax.rem(me, round_size)
    near_mine = copy_of * round_size + in_round
    bits = round_size.bit_length() - 1
    others = [copy_of] + [lax.rem(copy_of + step, copies) for step in range(1, copies)]
    far_first = sorted(range(1, near_count), key=lambda step: -step.bit_count())
    to_sens, to_ends, to_adj, to_near, to_far, to_within = range(6)

    turns = [(1 << bit) * (1 - 2 * lax.rem(me // (1 << bit), 2)) for bit in range(bits)]

    def near_spot(step):
        flips, other = step % round_size, step // round_size
        spot = me
        for bit in range(bits):
            if flips >> bit & 1:
                spot = spot + turns[bit]
        return {"ctx": spot, "dp": others[other]}

    def far_spot(step):
        return {"ctx": lax.rem(block + step, rounds) * round_size + in_round, "dp": copy_of}

    fetches = [
        pltpu.make_async_copy(source, target, fetch_sem.at[place])
        for place, (source, target) in enumerate(
            (
                (record_hbm, record_ref),
                (rate_hbm, rate_ref),
                (residue_hbm, residue_ref),
                (cotangent_hbm, cotangent_ref),
                (signal_hbm, signal_ref),
            )
        )
    ]
    for fetch in fetches:
        fetch.start()
    barrier = pltpu.get_barrier_semaphore()
    plane_count = CLUSTER * copies
    for step in range(1, plane_count):
        spot = near_spot(step // CLUSTER * round_size + step % CLUSTER)
        pl.semaphore_signal(barrier, inc=1, device_id=spot, device_id_type=MESH)

    def tell_lower(semaphore):
        for step in range(1, planes):

            @pl.when(plane - step >= 0)
            def _(step=step):
                spot = {"ctx": me - step * CLUSTER}
                pl.semaphore_signal(semaphore, inc=1, device_id=spot, device_id_type=MESH)

    higher_parts = [(copy, part) for copy in range(copies) for part in range(CLUSTER)]
    for step in range(1, planes):

        @pl.when(plane + step < planes)
        def _(step=step):
            spots = [{"ctx": me + step * CLUSTER}]
            if rounds == 1:
                spots = [
                    {"ctx": home + step * CLUSTER + part, "dp": copy}
                    for copy, part in higher_parts
                ]
            for spot in spots:
                pl.semaphore_signal(barrier, inc=1, device_id=spot, device_id_type=MESH)


    def wait_some(semaphore, count):
        @pl.when(count > 0)
        def _():
            pl.semaphore_wait(semaphore, count)

    lane = lax.broadcasted_iota(jnp.int32, (modes, length), 1).astype(F32)
    filter_lane = lax.broadcasted_iota(jnp.int32, (modes, filters), 1)
    tag_row = lax.broadcasted_iota(jnp.int32, (8, width), 0)
    row = lax.broadcasted_iota(jnp.int32, (length, length), 0)
    column = lax.broadcasted_iota(jnp.int32, (length, length), 1)
    for fetch in fetches[:3]:
        fetch.wait()
    ids = jnp.broadcast_to(record_ref[...].astype(F32), (length, length))
    first = ids[:8, :1]
    last = ids[:8, length - 1 :]
    in_first = (ids[:1] == first[:1]).astype(F32)
    in_last = (ids[:1] == last[:1]).astype(F32)
    tag = jnp.where(tag_row == 0, first, last)

    def group(index):
        return pl.ds(pl.multiple_of(index * width, width), width)

    def table_rows(index):
        return pl.ds(pl.multiple_of(index * modes, modes), modes)

    def edge_rows(index):
        return pl.ds(pl.multiple_of(index * 2 * modes, 2 * modes), 2 * modes)

    def column_of(ref, index):
        return jnp.sum(jnp.where(filter_lane == index, ref[...], 0.0), axis=1, keepdims=True)

    def norm_of(rate):
        double = 2.0 * rate
        series = 1.0 - double * (1.0 / 6.0) * (1.0 - double * (1.0 / 7.0))
        for divisor in (5.0, 4.0, 3.0, 2.0):
            series = 1.0 - double * (1.0 / divisor) * series
        return jnp.sqrt(double * series)

    def tagged(piece):
        return pl.ds(0, depth + 8) if piece == 0 else pl.ds(8 + piece * depth, depth)

    def plain(piece):
        return pl.ds(piece * depth, depth)

    def to_peer(source, target, send, recv, step):
        return pltpu.make_async_remote_copy(
            src_ref=source,
            dst_ref=target,
            send_sem=send_sem.at[send],
            recv_sem=recv,
            device_id={"ctx": home + lax.rem(mine + step, CLUSTER)},
            device_id_type=MESH,
        )

    def sens_copy(piece, step):
        peer = lax.rem(mine + step, CLUSTER)
        return to_peer(
            sens_out.at[peer, tagged(piece)],
            sens_in.at[mine, tagged(piece)],
            to_sens,
            sens_recv.at[piece],
            step,
        )

    def ends_copy(piece, step):
        peer = lax.rem(mine + step, CLUSTER)
        return to_peer(
            ends_out.at[peer, plain(piece)],
            ends_in.at[mine, plain(piece)],
            to_ends,
            ends_recv.at[0],
            step,
        )

    def adj_copy(piece, step):
        peer = lax.rem(mine + step, CLUSTER)
        return to_peer(
            adj_out.at[peer, plain(piece)],
            adj_in.at[mine, plain(piece)],
            to_adj,
            adj_recv.at[piece],
            step,
        )

    def wait_peers(ref, span, send, recv):
        several = ref.at[pl.ds(0, CLUSTER - 1), span]
        to_peer(several, several, send, recv, 1).wait_recv()

    def wait_sent(ref, send):
        several = ref.at[pl.ds(0, CLUSTER - 1)]
        to_peer(several, several, send, ends_recv.at[0], 1).wait_send()

    def sum_copy(piece, back):
        return pltpu.make_async_remote_copy(
            src_ref=sum_out.at[tagged(piece)],
            dst_ref=sum_in.at[back - 1, tagged(piece)],
            send_sem=sum_send.at[back - 1],
            recv_sem=sum_recv.at[piece, back - 1],
            device_id={"ctx": me - back * CLUSTER},
            device_id_type=MESH,
        )

    def prepare(index):
        rate = jnp.broadcast_to(column_of(rate_ref, index), (modes, width))
        rates[table_rows(index), :] = rate
        high, low = two_parts(jnp.exp(-rate * (lane + 1.0)) * in_first)
        starts[edge_rows(index), :] = jnp.concatenate([high, low], axis=0)

    def sense(index):
        both = dot(starts[edge_rows(index), :], cotangent_ref[:, group(index)])
        spot = pl.ds(pl.multiple_of(8 + lax.rem(index, share) * modes, 8), modes)
        sens_out[index // share, spot, :] = both[:modes] + both[modes:]

    def weigh(index, carry):
        norm = norm_of(rates[table_rows(index), :])
        weights[table_rows(index), :] = norm * column_of(residue_ref, index)
        return carry

    def end(index):
        rate = rates[table_rows(index), :]
        high, low = two_parts(jnp.exp(-rate * (length - 1.0 - lane)) * in_last)
        pair = jnp.concatenate([high, low], axis=0)
        edges[edge_rows(index), :] = pair
        both = dot(pair, signal_ref[:, group(index)])
        spot = pl.ds(pl.multiple_of(lax.rem(index, share) * modes, modes), modes)
        ends_out[index // share, spot, :] = both[:modes] + both[modes:]

    row_of = lax.broadcasted_iota(jnp.int32, (8, length), 0)

    def intra(index, carry):
        rate = rates[table_rows(index), :]
        products = dot(signal_ref[:, group(index)], cotangent_ref[:, group(index)], ((1,), (1,)))
        products = products * mask[...]
        parts = [products[:8]]
        for start in range(8, length, 8):
            parts.append(pltpu.roll(products[start : start + 8], length - start, 1))
        while len(parts) > 1:
            parts = [parts[i] + parts[i + 1] for i in range(0, len(parts), 2)]
        by_lag = parts[0]
        for bit in (1, 2, 4):
            moved = pltpu.roll(by_lag, length - bit, 1)
            by_lag = jnp.where((row_of & bit) != 0, moved, by_lag)
        by_lag = jnp.sum(by_lag, axis=0, keepdims=True)
        within[table_rows(index), :] = by_lag * jnp.exp(-rate * lane)
        return carry

    def near_by(index, carry):
        rate = rates[table_rows(index), :]
        weight = weights[table_rows(index), :]
        lags = jnp.sum(weight * jnp.exp(-rate * lane), axis=0, keepdims=True)
        spread = pltpu.roll(
            jnp.broadcast_to(lags, (length, length)), 0, 1, stride=1, stride_axis=0
        )
        kernel_now = (spread * mask[...]).astype(BF16)
        local[:, group(index)] = dot(kernel_now, cotangent_ref[:, group(index)])
        return carry

    for part in range(CLUSTER):
        sens_out[part, :8, :] = tag
    for back in BACKS:

        @pl.when(me + back * CLUSTER >= shards)
        def _(back=back):
            sum_in[back - 1] = jnp.full(sum_in.shape[1:], -1.0, F32)

    for index in range(filters):
        prepare(index)
    fetches[3].wait()
    for piece in range(PIECES):
        for step in (2, 1, 3, 0):
            base = lax.rem(mine + step, CLUSTER) * share + piece * batch
            for index in range(batch):
                sense(base + index)
        if piece == 0:
            pl.semaphore_wait(barrier, plane_count - 1 + plane * (plane_count if rounds == 1 else 1))
            tell_lower(entered.at[0])
        for step in (3, 1, 2):
            sens_copy(piece, step).start()
        sens_in[mine, tagged(piece), :] = sens_out[mine, tagged(piece), :]
    mask[...] = jnp.where((ids == ids.T) & (column >= row), 1.0, 0.0)
    fetches[4].wait()
    for piece in range(PIECES):
        for step in (2, 1, 3, 0):
            base = lax.rem(mine + step, CLUSTER) * share + piece * batch
            for index in range(batch):
                end(base + index)
    for piece in range(PIECES):
        for step in (3, 1, 2):
            ends_copy(piece, step).start()
        ends_in[mine, plain(piece), :] = ends_out[mine, plain(piece), :]

    def decay_of(piece):
        start = pl.multiple_of(mine * rows + piece * depth, 8)
        return jnp.exp(-rates[pl.ds(start, depth), :] * float(length))

    lax.fori_loop(0, filters // 2, intra, 0, unroll=16)
    lax.fori_loop(0, filters, weigh, 0, unroll=16)

    for piece in range(PIECES):
        if piece == 2:
            lax.fori_loop(filters // 2, filters, intra, 0, unroll=16)
            for part in range(CLUSTER):
                within_out[part] = row_sums(within[part * rows : (part + 1) * rows, :])
            for step in (3, 1, 2):
                peer = lax.rem(mine + step, CLUSTER)
                to_peer(
                    within_out.at[peer], within_in.at[mine], to_within, within_recv.at[0], step
                ).start()
            within_in[mine] = within_out[mine]
        wait_peers(sens_in, tagged(piece), to_sens, sens_recv.at[piece])
        decay = decay_of(piece)
        firsts = [sens_in[place, 0:1, :] for place in range(CLUSTER)]
        lasts = [sens_in[place, 1:2, :] for place in range(CLUSTER)]
        span = pl.ds(8 + piece * depth, depth)
        values = []
        value = jnp.zeros((depth, width), F32)
        for place in range(CLUSTER - 1, -1, -1):
            values.append(value)
            value = jnp.where(firsts[place] == lasts[place], decay * value, 0.0)
            value = sens_in[place, span, :] + value
            if place:
                value = jnp.where(firsts[place] == lasts[place - 1], value, 0.0)
        sum_out[span, :] = value
        if piece == 0:
            sum_out[:8, :] = sens_in[0, :8, :]
        for back in BACKS:

            @pl.when(me - back * CLUSTER >= 0)
            def _(piece=piece, back=back):
                sum_copy(piece, back).start()

        for place, value in enumerate(reversed(values)):
            adj_out[place, plain(piece), :] = value


    for piece in range(PIECES):
        for back in BACKS:

            @pl.when(me + back * CLUSTER < shards)
            def _(piece=piece, back=back):
                sum_copy(piece, back).wait_recv()

        decay = decay_of(piece)
        span = pl.ds(8 + piece * depth, depth)
        fourth = decay * decay
        fourth = fourth * fourth
        moved = [sum_in[0, span, :], fourth * sum_in[1, span, :]]
        for place in range(CLUSTER - 1, -1, -1):
            value = adj_out[place, plain(piece), :]
            for back in BACKS:
                hit = sum_in[back - 1, 0:1, :] == sens_in[place, 1:2, :]
                value = value + jnp.where(hit, moved[back - 1], 0.0)
            adj_out[place, plain(piece), :] = value
            if place:
                moved = [decay * value for value in moved]
        for step in (3, 1, 2):
            adj_copy(piece, step).start()
        adj_in[mine, plain(piece), :] = adj_out[mine, plain(piece), :]

    wait_some(entered.at[0], planes - 1 - plane)
    wait_peers(ends_in, pl.ds(0, rows), to_ends, ends_recv.at[0])
    product = ends_in[0] * adj_out[0]
    for place in range(1, CLUSTER):
        product = product + ends_in[place] * adj_out[place]
    wait_peers(within_in, pl.ds(0, 1), to_within, within_recv.at[0])
    terms = row_sums(product)
    for place in range(CLUSTER):
        terms = terms + within_in[place]
    near_out[0] = terms

    def near_copy(step):
        return pltpu.make_async_remote_copy(
            src_ref=near_out.at[0],
            dst_ref=near_in.at[near_mine],
            send_sem=send_sem.at[to_near],
            recv_sem=reduce_recv.at[0],
            device_id=near_spot(step),
            device_id_type=MESH,
        )

    def far_copy(step):
        return pltpu.make_async_remote_copy(
            src_ref=far_out,
            dst_ref=far_in.at[block],
            send_sem=send_sem.at[to_far],
            recv_sem=reduce_recv.at[1],
            device_id=far_spot(step),
            device_id_type=MESH,
        )

    def all_of(ref, count, send, recv):
        several = ref.at[pl.ds(0, count)]
        return to_peer(several, several, send, recv, 1)

    near_all = all_of(near_in, near_count - 1, to_near, reduce_recv.at[0])
    far_all = all_of(far_in, rounds - 1, to_far, reduce_recv.at[1]) if rounds > 1 else None

    for step in far_first:
        near_copy(step).start()
    near_in[near_mine] = near_out[0]
    norm_ref[...] = norm_of(rate_ref[...]) * scale

    lax.fori_loop(0, filters, near_by, 0, unroll=16)

    def gather_near():
        near_all.wait_recv()
        for part in range(CLUSTER):
            total = near_in[part]
            for rank in range(part + CLUSTER, near_count, CLUSTER):
                total = total + near_in[rank]
            total_ref[part : part + 1, :] = total

    if rounds > 1:
        gather_near()
        far_out[...] = total_ref[...]
        for step in range(1, rounds):
            far_copy(step).start()
        far_in[block] = far_out[...]

    def finish(index):
        high_low = edges[edge_rows(index), :]
        spot = pl.ds(pl.multiple_of(lax.rem(index, share) * modes, modes), modes)
        adjoint = adj_in[index // share, spot, :]
        adj_high, adj_low = two_parts(weights[table_rows(index), :] * adjoint)
        left = jnp.concatenate([high_low, high_low[:modes]], axis=0)
        right = jnp.concatenate([adj_high, adj_high, adj_low], axis=0)
        carried = dot(left, right, ((0,), (0,)))
        grad_ref[:, group(index)] = (local[:, group(index)] + carried).astype(BF16)

    for piece in range(PIECES):
        wait_peers(adj_in, plain(piece), to_adj, adj_recv.at[piece])

        def finish_one(turn, carry, piece=piece):
            finish(turn // batch * share + piece * batch + lax.rem(turn, batch))
            return carry

        lax.fori_loop(0, CLUSTER * batch, finish_one, 0, unroll=8)

    if rounds > 1:
        far_all.wait_recv()
        far_total = far_in[0]
        for rank in range(1, rounds):
            far_total = far_total + far_in[rank]
        total_ref[...] = far_total
    else:
        gather_near()

    wait_sent(sens_out, to_sens)
    wait_sent(ends_out, to_ends)
    wait_sent(adj_out, to_adj)
    wait_sent(within_out, to_within)
    near_all.wait_send()
    if rounds > 1:
        far_all.wait_send()
    for back in BACKS:

        @pl.when(me - back * CLUSTER >= 0)
        def _(back=back):
            pltpu.make_async_remote_copy(
                src_ref=sum_out,
                dst_ref=sum_in.at[back - 1],
                send_sem=sum_send.at[back - 1],
                recv_sem=sum_recv.at[0, back - 1],
                device_id={"ctx": me - back * CLUSTER},
                device_id_type=MESH,
            ).wait_send()


def store(grad_ref, total_ref, norm_ref, grad_hbm, term_hbm, term_ref, sems):
    write_grad = pltpu.make_async_copy(grad_ref, grad_hbm, sems.at[0])
    write_grad.start()
    modes, filters = norm_ref.shape
    parts, rows = total_ref.shape
    share = filters // parts
    row = lax.broadcasted_iota(jnp.int32, (rows, filters), 0)
    column = lax.broadcasted_iota(jnp.int32, (rows, filters), 1)
    lane = lax.broadcasted_iota(jnp.int32, (modes, rows), 1)
    mode = lax.broadcasted_iota(jnp.int32, (modes, rows), 0)
    own = (lane & (modes - 1)) == mode
    total = jnp.zeros((3 * modes, filters), F32)
    for part in range(parts):
        spread = jnp.where(own, total_ref[part : part + 1, :], 0.0)
        high, rest = spread.astype(BF16), spread - spread.astype(BF16).astype(F32)
        middle, low = two_parts(rest)
        start = (column - part * share) * modes
        pick = jnp.where((row >= start) & (row < start + modes), 1.0, 0.0).astype(BF16)
        total = total + dot(jnp.concatenate([high, middle, low], axis=0), pick)
    total = total[:modes] + (total[modes : 2 * modes] + total[2 * modes :])
    term_ref[...] = norm_ref[...] * total
    write_term = pltpu.make_async_copy(term_ref, term_hbm, sems.at[1])
    write_term.start()
    write_term.wait()
    write_grad.wait()


def body(signal, cotangent, record_id, rate, residue):
    length, width = signal.shape[1:]
    filters, modes = rate.shape
    shards = lax.axis_size("ctx")
    group_width = width // filters
    rows = filters // CLUSTER * modes
    sequences = signal.shape[0] * lax.axis_size("dp")
    scale = 1.0 / math.sqrt(sequences * length * shards * group_width)
    copies = lax.axis_size("dp")
    near_count = round_of(shards, copies) * copies
    rounds = shards // round_of(shards, copies)
    hbm = pl.BlockSpec(memory_space=pltpu.HBM)
    vmem = pl.BlockSpec(memory_space=pltpu.VMEM)
    in_hbm = functools.partial(pltpu.with_memory_space_constraint, memory_space=pltpu.HBM)
    in_vmem = functools.partial(pltpu.with_memory_space_constraint, memory_space=pltpu.VMEM)
    dma = pltpu.SemaphoreType.DMA
    grad, total, norm = pl.pallas_call(
        functools.partial(kernel, filters, modes, shards, scale, copies),
        out_shape=(
            pltpu.VMEM((length, width), BF16),
            pltpu.VMEM((CLUSTER, rows), F32),
            pltpu.VMEM((modes, filters), F32),
        ),
        in_specs=[hbm] * 5,
        out_specs=(vmem, vmem, vmem),
        scratch_shapes=[
            pltpu.VMEM((length, width), BF16),
            pltpu.VMEM((length, width), BF16),
            pltpu.VMEM(record_id.shape, jnp.int32),
            pltpu.VMEM((modes, filters), F32),
            pltpu.VMEM((modes, filters), F32),
            pltpu.VMEM((filters * modes, group_width), F32),
            pltpu.VMEM((filters * modes, group_width), F32),
            pltpu.VMEM((length, length), F32),
            pltpu.VMEM((filters * 2 * modes, length), BF16),
            pltpu.VMEM((filters * 2 * modes, length), BF16),
            pltpu.VMEM((length, width), F32),
            pltpu.VMEM((filters * modes, length), F32),
            pltpu.VMEM((CLUSTER, 1, rows), F32),
            pltpu.VMEM((CLUSTER, 1, rows), F32),
            pltpu.VMEM((CLUSTER, rows + 8, group_width), F32),
            pltpu.VMEM((CLUSTER, rows + 8, group_width), F32),
            pltpu.VMEM((CLUSTER, rows, group_width), F32),
            pltpu.VMEM((CLUSTER, rows, group_width), F32),
            pltpu.VMEM((rows + 8, group_width), F32),
            pltpu.VMEM((2, rows + 8, group_width), F32),
            pltpu.VMEM((CLUSTER, rows, group_width), F32),
            pltpu.VMEM((CLUSTER, rows, group_width), F32),
            pltpu.VMEM((1, 1, rows), F32),
            pltpu.VMEM((near_count, 1, rows), F32),
            pltpu.VMEM((CLUSTER, rows), F32),
            pltpu.VMEM((rounds, CLUSTER, rows), F32),
            dma((6,)),
            dma((2,)),
            dma((PIECES,)),
            dma((1,)),
            dma((1,)),
            dma((PIECES, 2)),
            dma((PIECES,)),
            dma((2,)),
            dma((5,)),
            pltpu.SemaphoreType.REGULAR((1,)),
        ],
        compiler_params=pltpu.CompilerParams(
            collective_id=0, has_side_effects=True, vmem_limit_bytes=52 << 20
        ),
    )(*(in_hbm(x) for x in (signal[0], cotangent[0], record_id, rate.T, residue.T)))
    grad, terms = pl.pallas_call(
        store,
        out_shape=(
            jax.ShapeDtypeStruct((length, width), BF16),
            jax.ShapeDtypeStruct((modes, filters), F32),
        ),
        in_specs=[vmem, vmem, vmem],
        out_specs=(hbm, hbm),
        scratch_shapes=[pltpu.VMEM((modes, filters), F32), dma((2,))],
    )(in_vmem(grad), in_vmem(total), in_vmem(norm))
    return grad[None], terms.T


def solution(mesh):
    return jax.shard_map(
        body,
        mesh=mesh,
        in_specs=(P("dp", "ctx", None), P("dp", "ctx", None), P("dp", "ctx"), P(), P()),
        out_specs=(P("dp", "ctx", None), P()),
        check_vma=False,
    )
```

```python
import functools
import math

import jax
import jax.numpy as jnp
from jax import lax
from jax.experimental import pallas as pl
from jax.experimental.pallas import tpu as pltpu
from jax.sharding import PartitionSpec as P

CLUSTER = 4
PIECES = 4
BACKS = (1, 2)
ONE_ROUND = 64
MESH = pl.DeviceIdType.MESH
F32 = jnp.float32
BF16 = jnp.bfloat16


def two_parts(table):
    high = table.astype(BF16)
    return high, (table - high.astype(F32)).astype(BF16)


def dot(left, right, contract=((1,), (0,))):
    return lax.dot_general(left, right, (contract, ((), ())), preferred_element_type=F32)


def row_sums(table):
    return jnp.sum(table.T, axis=0, keepdims=True)


def round_of(shards, copies):
    return shards if shards * copies <= ONE_ROUND else CLUSTER


def kernel(
    filters,
    modes,
    shards,
    scale,
    copies,
    signal_hbm,
    cotangent_hbm,
    record_hbm,
    rate_hbm,
    residue_hbm,
    grad_ref,
    total_ref,
    norm_ref,
    signal_ref,
    cotangent_ref,
    record_ref,
    rate_ref,
    residue_ref,
    rates,
    weights,
    mask,
    edges,
    starts,
    local,
    within,
    within_out,
    within_in,
    sens_out,
    sens_in,
    ends_out,
    ends_in,
    sum_out,
    sum_in,
    adj_out,
    adj_in,
    near_out,
    near_in,
    far_out,
    far_in,
    send_sem,
    sum_send,
    sens_recv,
    ends_recv,
    within_recv,
    sum_recv,
    adj_recv,
    reduce_recv,
    fetch_sem,
    entered,
):
    length = signal_ref.shape[0]
    width = signal_ref.shape[1] // filters
    share = filters // CLUSTER
    rows = share * modes
    depth = rows // PIECES
    batch = share // PIECES
    me = lax.axis_index("ctx")
    mine = lax.rem(me, CLUSTER)
    home = me - mine
    copy_of = lax.axis_index("dp")
    planes = shards // CLUSTER
    plane = me // CLUSTER
    round_size = round_of(shards, copies)
    near_count = round_size * copies
    rounds = shards // round_size
    block = me // round_size
    in_round = lax.rem(me, round_size)
    near_mine = copy_of * round_size + in_round
    bits = round_size.bit_length() - 1
    others = [copy_of] + [lax.rem(copy_of + step, copies) for step in range(1, copies)]
    far_first = sorted(range(1, near_count), key=lambda step: -step.bit_count())
    to_sens, to_ends, to_adj, to_near, to_far, to_within = range(6)

    turns = [(1 << bit) * (1 - 2 * lax.rem(me // (1 << bit), 2)) for bit in range(bits)]

    def near_spot(step):
        flips, other = step % round_size, step // round_size
        spot = me
        for bit in range(bits):
            if flips >> bit & 1:
                spot = spot + turns[bit]
        return {"ctx": spot, "dp": others[other]}

    def far_spot(step):
        return {"ctx": lax.rem(block + step, rounds) * round_size + in_round, "dp": copy_of}

    fetches = [
        pltpu.make_async_copy(source, target, fetch_sem.at[place])
        for place, (source, target) in enumerate(
            (
                (record_hbm, record_ref),
                (rate_hbm, rate_ref),
                (residue_hbm, residue_ref),
                (cotangent_hbm, cotangent_ref),
                (signal_hbm, signal_ref),
            )
        )
    ]
    for fetch in fetches:
        fetch.start()
    barrier = pltpu.get_barrier_semaphore()
    plane_count = CLUSTER * copies
    for step in range(1, plane_count):
        spot = near_spot(step // CLUSTER * round_size + step % CLUSTER)
        pl.semaphore_signal(barrier, inc=1, device_id=spot, device_id_type=MESH)

    def tell_lower(semaphore):
        for step in range(1, planes):

            @pl.when(plane - step >= 0)
            def _(step=step):
                spot = {"ctx": me - step * CLUSTER}
                pl.semaphore_signal(semaphore, inc=1, device_id=spot, device_id_type=MESH)

    higher_parts = [(copy, part) for copy in range(copies) for part in range(CLUSTER)]
    for step in range(1, planes):

        @pl.when(plane + step < planes)
        def _(step=step):
            spots = [{"ctx": me + step * CLUSTER}]
            if rounds == 1:
                spots = [
                    {"ctx": home + step * CLUSTER + part, "dp": copy}
                    for copy, part in higher_parts
                ]
            for spot in spots:
                pl.semaphore_signal(barrier, inc=1, device_id=spot, device_id_type=MESH)


    def wait_some(semaphore, count):
        @pl.when(count > 0)
        def _():
            pl.semaphore_wait(semaphore, count)

    lane = lax.broadcasted_iota(jnp.int32, (modes, length), 1).astype(F32)
    filter_lane = lax.broadcasted_iota(jnp.int32, (modes, filters), 1)
    tag_row = lax.broadcasted_iota(jnp.int32, (8, width), 0)
    row = lax.broadcasted_iota(jnp.int32, (length, length), 0)
    column = lax.broadcasted_iota(jnp.int32, (length, length), 1)
    for fetch in fetches[:3]:
        fetch.wait()
    ids = jnp.broadcast_to(record_ref[...].astype(F32), (length, length))
    first = ids[:8, :1]
    last = ids[:8, length - 1 :]
    in_first = (ids[:1] == first[:1]).astype(F32)
    in_last = (ids[:1] == last[:1]).astype(F32)
    tag = jnp.where(tag_row == 0, first, last)

    def group(index):
        return pl.ds(pl.multiple_of(index * width, width), width)

    def table_rows(index):
        return pl.ds(pl.multiple_of(index * modes, modes), modes)

    def edge_rows(index):
        return pl.ds(pl.multiple_of(index * 2 * modes, 2 * modes), 2 * modes)

    def column_of(ref, index):
        return jnp.sum(jnp.where(filter_lane == index, ref[...], 0.0), axis=1, keepdims=True)

    def norm_of(rate):
        double = 2.0 * rate
        series = 1.0 - double * (1.0 / 6.0) * (1.0 - double * (1.0 / 7.0))
        for divisor in (5.0, 4.0, 3.0, 2.0):
            series = 1.0 - double * (1.0 / divisor) * series
        return jnp.sqrt(double * series)

    def tagged(piece):
        return pl.ds(0, depth + 8) if piece == 0 else pl.ds(8 + piece * depth, depth)

    def plain(piece):
        return pl.ds(piece * depth, depth)

    def to_peer(source, target, send, recv, step):
        return pltpu.make_async_remote_copy(
            src_ref=source,
            dst_ref=target,
            send_sem=send_sem.at[send],
            recv_sem=recv,
            device_id={"ctx": home + lax.rem(mine + step, CLUSTER)},
            device_id_type=MESH,
        )

    def sens_copy(piece, step):
        peer = lax.rem(mine + step, CLUSTER)
        return to_peer(
            sens_out.at[peer, tagged(piece)],
            sens_in.at[mine, tagged(piece)],
            to_sens,
            sens_recv.at[piece],
            step,
        )

    def adj_copy(piece, step):
        peer = lax.rem(mine + step, CLUSTER)
        return to_peer(
            adj_out.at[peer, plain(piece)],
            adj_in.at[mine, plain(piece)],
            to_adj,
            adj_recv.at[piece],
            step,
        )

    def wait_peers(ref, span, send, recv):
        several = ref.at[pl.ds(0, CLUSTER - 1), span]
        to_peer(several, several, send, recv, 1).wait_recv()

    def wait_sent(ref, send):
        several = ref.at[pl.ds(0, CLUSTER - 1)]
        to_peer(several, several, send, ends_recv.at[0], 1).wait_send()

    def sum_copy(piece, back):
        return pltpu.make_async_remote_copy(
            src_ref=sum_out.at[tagged(piece)],
            dst_ref=sum_in.at[back - 1, tagged(piece)],
            send_sem=sum_send.at[back - 1],
            recv_sem=sum_recv.at[piece, back - 1],
            device_id={"ctx": me - back * CLUSTER},
            device_id_type=MESH,
        )

    def prepare(index):
        rate = jnp.broadcast_to(column_of(rate_ref, index), (modes, width))
        rates[table_rows(index), :] = rate
        high, low = two_parts(jnp.exp(-rate * (lane + 1.0)) * in_first)
        starts[edge_rows(index), :] = jnp.concatenate([high, low], axis=0)

    def sense(index):
        both = dot(starts[edge_rows(index), :], cotangent_ref[:, group(index)])
        spot = pl.ds(pl.multiple_of(8 + lax.rem(index, share) * modes, 8), modes)
        sens_out[index // share, spot, :] = both[:modes] + both[modes:]

    def weigh(index, carry):
        norm = norm_of(rates[table_rows(index), :])
        weights[table_rows(index), :] = norm * column_of(residue_ref, index)
        return carry

    def end(index):
        rate = rates[table_rows(index), :]
        high, low = two_parts(jnp.exp(-rate * (length - 1.0 - lane)) * in_last)
        pair = jnp.concatenate([high, low], axis=0)
        edges[edge_rows(index), :] = pair
        both = dot(pair, signal_ref[:, group(index)])
        spot = pl.ds(pl.multiple_of(lax.rem(index, share) * modes, modes), modes)
        ends_out[index // share, spot, :] = both[:modes] + both[modes:]

    row_of = lax.broadcasted_iota(jnp.int32, (8, length), 0)

    def intra(index, carry):
        rate = rates[table_rows(index), :]
        products = dot(signal_ref[:, group(index)], cotangent_ref[:, group(index)], ((1,), (1,)))
        products = products * mask[...]
        parts = [products[:8]]
        for start in range(8, length, 8):
            parts.append(pltpu.roll(products[start : start + 8], length - start, 1))
        while len(parts) > 1:
            parts = [parts[i] + parts[i + 1] for i in range(0, len(parts), 2)]
        by_lag = parts[0]
        for bit in (1, 2, 4):
            moved = pltpu.roll(by_lag, length - bit, 1)
            by_lag = jnp.where((row_of & bit) != 0, moved, by_lag)
        by_lag = jnp.sum(by_lag, axis=0, keepdims=True)
        within[table_rows(index), :] = by_lag * jnp.exp(-rate * lane)
        return carry

    def near_by(index, carry):
        rate = rates[table_rows(index), :]
        weight = weights[table_rows(index), :]
        lags = jnp.sum(weight * jnp.exp(-rate * lane), axis=0, keepdims=True)
        spread = pltpu.roll(
            jnp.broadcast_to(lags, (length, length)), 0, 1, stride=1, stride_axis=0
        )
        kernel_now = (spread * mask[...]).astype(BF16)
        local[:, group(index)] = dot(kernel_now, cotangent_ref[:, group(index)])
        return carry

    for part in range(CLUSTER):
        sens_out[part, :8, :] = tag
    for back in BACKS:

        @pl.when(me + back * CLUSTER >= shards)
        def _(back=back):
            sum_in[back - 1] = jnp.full(sum_in.shape[1:], -1.0, F32)

    for index in range(filters):
        prepare(index)
    fetches[3].wait()
    for piece in range(PIECES):
        for step in (2, 1, 3, 0):
            base = lax.rem(mine + step, CLUSTER) * share + piece * batch
            for index in range(batch):
                sense(base + index)
        if piece == 0:
            pl.semaphore_wait(barrier, plane_count - 1 + plane * (plane_count if rounds == 1 else 1))
            tell_lower(entered.at[0])
        for step in (3, 1, 2):
            sens_copy(piece, step).start()
        sens_in[mine, tagged(piece), :] = sens_out[mine, tagged(piece), :]
    mask[...] = jnp.where((ids == ids.T) & (column >= row), 1.0, 0.0)
    fetches[4].wait()
    for piece in range(PIECES):
        for step in (2, 1, 3, 0):
            base = lax.rem(mine + step, CLUSTER) * share + piece * batch
            for index in range(batch):
                end(base + index)
    for step in (3, 1, 2):
        peer = lax.rem(mine + step, CLUSTER)
        to_peer(ends_out.at[peer], ends_in.at[mine], to_ends, ends_recv.at[0], step).start()
    for piece in range(PIECES):
        ends_in[mine, plain(piece), :] = ends_out[mine, plain(piece), :]

    def decay_of(piece):
        start = pl.multiple_of(mine * rows + piece * depth, 8)
        return jnp.exp(-rates[pl.ds(start, depth), :] * float(length))

    lax.fori_loop(0, filters // 2, intra, 0, unroll=16)

    for piece in range(PIECES):
        if piece == 1:
            lax.fori_loop(filters // 2, filters, intra, 0, unroll=16)
            for part in range(CLUSTER):
                within_out[part] = row_sums(within[part * rows : (part + 1) * rows, :])
            for step in (3, 1, 2):
                peer = lax.rem(mine + step, CLUSTER)
                to_peer(
                    within_out.at[peer], within_in.at[mine], to_within, within_recv.at[0], step
                ).start()
            within_in[mine] = within_out[mine]
        wait_peers(sens_in, tagged(piece), to_sens, sens_recv.at[piece])
        decay = decay_of(piece)
        firsts = [sens_in[place, 0:1, :] for place in range(CLUSTER)]
        lasts = [sens_in[place, 1:2, :] for place in range(CLUSTER)]
        span = pl.ds(8 + piece * depth, depth)
        values = []
        value = jnp.zeros((depth, width), F32)
        for place in range(CLUSTER - 1, -1, -1):
            values.append(value)
            value = jnp.where(firsts[place] == lasts[place], decay * value, 0.0)
            value = sens_in[place, span, :] + value
            if place:
                value = jnp.where(firsts[place] == lasts[place - 1], value, 0.0)
        sum_out[span, :] = value
        if piece == 0:
            sum_out[:8, :] = sens_in[0, :8, :]
        for back in BACKS:

            @pl.when(me - back * CLUSTER >= 0)
            def _(piece=piece, back=back):
                sum_copy(piece, back).start()

        for place, value in enumerate(reversed(values)):
            adj_out[place, plain(piece), :] = value


    for piece in range(PIECES):
        for back in BACKS:

            @pl.when(me + back * CLUSTER < shards)
            def _(piece=piece, back=back):
                sum_copy(piece, back).wait_recv()

        decay = decay_of(piece)
        span = pl.ds(8 + piece * depth, depth)
        fourth = decay * decay
        fourth = fourth * fourth
        moved = [sum_in[0, span, :], fourth * sum_in[1, span, :]]
        for place in range(CLUSTER - 1, -1, -1):
            value = adj_out[place, plain(piece), :]
            for back in BACKS:
                hit = sum_in[back - 1, 0:1, :] == sens_in[place, 1:2, :]
                value = value + jnp.where(hit, moved[back - 1], 0.0)
            adj_out[place, plain(piece), :] = value
            if place:
                moved = [decay * value for value in moved]
        for step in (3, 1, 2):
            adj_copy(piece, step).start()
        adj_in[mine, plain(piece), :] = adj_out[mine, plain(piece), :]

    wait_some(entered.at[0], planes - 1 - plane)
    wait_peers(ends_in, pl.ds(0, rows), to_ends, ends_recv.at[0])
    product = ends_in[0] * adj_out[0]
    for place in range(1, CLUSTER):
        product = product + ends_in[place] * adj_out[place]
    wait_peers(within_in, pl.ds(0, 1), to_within, within_recv.at[0])
    terms = row_sums(product)
    for place in range(CLUSTER):
        terms = terms + within_in[place]
    near_out[0] = terms

    def near_copy(step):
        return pltpu.make_async_remote_copy(
            src_ref=near_out.at[0],
            dst_ref=near_in.at[near_mine],
            send_sem=send_sem.at[to_near],
            recv_sem=reduce_recv.at[0],
            device_id=near_spot(step),
            device_id_type=MESH,
        )

    def far_copy(step):
        return pltpu.make_async_remote_copy(
            src_ref=far_out,
            dst_ref=far_in.at[block],
            send_sem=send_sem.at[to_far],
            recv_sem=reduce_recv.at[1],
            device_id=far_spot(step),
            device_id_type=MESH,
        )

    def all_of(ref, count, send, recv):
        several = ref.at[pl.ds(0, count)]
        return to_peer(several, several, send, recv, 1)

    near_all = all_of(near_in, near_count - 1, to_near, reduce_recv.at[0])
    far_all = all_of(far_in, rounds - 1, to_far, reduce_recv.at[1]) if rounds > 1 else None

    for step in far_first:
        near_copy(step).start()
    near_in[near_mine] = near_out[0]
    norm_ref[...] = norm_of(rate_ref[...]) * scale

    lax.fori_loop(0, filters, weigh, 0, unroll=16)
    lax.fori_loop(0, filters, near_by, 0, unroll=16)

    def gather_near():
        near_all.wait_recv()
        for part in range(CLUSTER):
            total = near_in[part]
            for rank in range(part + CLUSTER, near_count, CLUSTER):
                total = total + near_in[rank]
            total_ref[part : part + 1, :] = total

    if rounds > 1:
        gather_near()
        far_out[...] = total_ref[...]
        for step in range(1, rounds):
            far_copy(step).start()
        far_in[block] = far_out[...]

    def finish(index):
        high_low = edges[edge_rows(index), :]
        spot = pl.ds(pl.multiple_of(lax.rem(index, share) * modes, modes), modes)
        adjoint = adj_in[index // share, spot, :]
        adj_high, adj_low = two_parts(weights[table_rows(index), :] * adjoint)
        left = jnp.concatenate([high_low, high_low[:modes]], axis=0)
        right = jnp.concatenate([adj_high, adj_high, adj_low], axis=0)
        carried = dot(left, right, ((0,), (0,)))
        grad_ref[:, group(index)] = (local[:, group(index)] + carried).astype(BF16)

    for piece in range(PIECES):
        wait_peers(adj_in, plain(piece), to_adj, adj_recv.at[piece])

        def finish_one(turn, carry, piece=piece):
            finish(turn // batch * share + piece * batch + lax.rem(turn, batch))
            return carry

        lax.fori_loop(0, CLUSTER * batch, finish_one, 0, unroll=8)

    if rounds > 1:
        far_all.wait_recv()
        far_total = far_in[0]
        for rank in range(1, rounds):
            far_total = far_total + far_in[rank]
        total_ref[...] = far_total
    else:
        gather_near()

    wait_sent(sens_out, to_sens)
    wait_sent(ends_out, to_ends)
    wait_sent(adj_out, to_adj)
    wait_sent(within_out, to_within)
    near_all.wait_send()
    if rounds > 1:
        far_all.wait_send()
    for back in BACKS:

        @pl.when(me - back * CLUSTER >= 0)
        def _(back=back):
            pltpu.make_async_remote_copy(
                src_ref=sum_out,
                dst_ref=sum_in.at[back - 1],
                send_sem=sum_send.at[back - 1],
                recv_sem=sum_recv.at[0, back - 1],
                device_id={"ctx": me - back * CLUSTER},
                device_id_type=MESH,
            ).wait_send()


def store(grad_ref, total_ref, norm_ref, grad_hbm, term_hbm, term_ref, sems):
    write_grad = pltpu.make_async_copy(grad_ref, grad_hbm, sems.at[0])
    write_grad.start()
    modes, filters = norm_ref.shape
    parts, rows = total_ref.shape
    share = filters // parts
    row = lax.broadcasted_iota(jnp.int32, (rows, filters), 0)
    column = lax.broadcasted_iota(jnp.int32, (rows, filters), 1)
    lane = lax.broadcasted_iota(jnp.int32, (modes, rows), 1)
    mode = lax.broadcasted_iota(jnp.int32, (modes, rows), 0)
    own = (lane & (modes - 1)) == mode
    total = jnp.zeros((3 * modes, filters), F32)
    for part in range(parts):
        spread = jnp.where(own, total_ref[part : part + 1, :], 0.0)
        high, rest = spread.astype(BF16), spread - spread.astype(BF16).astype(F32)
        middle, low = two_parts(rest)
        start = (column - part * share) * modes
        pick = jnp.where((row >= start) & (row < start + modes), 1.0, 0.0).astype(BF16)
        total = total + dot(jnp.concatenate([high, middle, low], axis=0), pick)
    total = total[:modes] + (total[modes : 2 * modes] + total[2 * modes :])
    term_ref[...] = norm_ref[...] * total
    write_term = pltpu.make_async_copy(term_ref, term_hbm, sems.at[1])
    write_term.start()
    write_term.wait()
    write_grad.wait()


def body(signal, cotangent, record_id, rate, residue):
    length, width = signal.shape[1:]
    filters, modes = rate.shape
    shards = lax.axis_size("ctx")
    group_width = width // filters
    rows = filters // CLUSTER * modes
    sequences = signal.shape[0] * lax.axis_size("dp")
    scale = 1.0 / math.sqrt(sequences * length * shards * group_width)
    copies = lax.axis_size("dp")
    near_count = round_of(shards, copies) * copies
    rounds = shards // round_of(shards, copies)
    hbm = pl.BlockSpec(memory_space=pltpu.HBM)
    vmem = pl.BlockSpec(memory_space=pltpu.VMEM)
    in_hbm = functools.partial(pltpu.with_memory_space_constraint, memory_space=pltpu.HBM)
    in_vmem = functools.partial(pltpu.with_memory_space_constraint, memory_space=pltpu.VMEM)
    dma = pltpu.SemaphoreType.DMA
    grad, total, norm = pl.pallas_call(
        functools.partial(kernel, filters, modes, shards, scale, copies),
        out_shape=(
            pltpu.VMEM((length, width), BF16),
            pltpu.VMEM((CLUSTER, rows), F32),
            pltpu.VMEM((modes, filters), F32),
        ),
        in_specs=[hbm] * 5,
        out_specs=(vmem, vmem, vmem),
        scratch_shapes=[
            pltpu.VMEM((length, width), BF16),
            pltpu.VMEM((length, width), BF16),
            pltpu.VMEM(record_id.shape, jnp.int32),
            pltpu.VMEM((modes, filters), F32),
            pltpu.VMEM((modes, filters), F32),
            pltpu.VMEM((filters * modes, group_width), F32),
            pltpu.VMEM((filters * modes, group_width), F32),
            pltpu.VMEM((length, length), F32),
            pltpu.VMEM((filters * 2 * modes, length), BF16),
            pltpu.VMEM((filters * 2 * modes, length), BF16),
            pltpu.VMEM((length, width), F32),
            pltpu.VMEM((filters * modes, length), F32),
            pltpu.VMEM((CLUSTER, 1, rows), F32),
            pltpu.VMEM((CLUSTER, 1, rows), F32),
            pltpu.VMEM((CLUSTER, rows + 8, group_width), F32),
            pltpu.VMEM((CLUSTER, rows + 8, group_width), F32),
            pltpu.VMEM((CLUSTER, rows, group_width), F32),
            pltpu.VMEM((CLUSTER, rows, group_width), F32),
            pltpu.VMEM((rows + 8, group_width), F32),
            pltpu.VMEM((2, rows + 8, group_width), F32),
            pltpu.VMEM((CLUSTER, rows, group_width), F32),
            pltpu.VMEM((CLUSTER, rows, group_width), F32),
            pltpu.VMEM((1, 1, rows), F32),
            pltpu.VMEM((near_count, 1, rows), F32),
            pltpu.VMEM((CLUSTER, rows), F32),
            pltpu.VMEM((rounds, CLUSTER, rows), F32),
            dma((6,)),
            dma((2,)),
            dma((PIECES,)),
            dma((1,)),
            dma((1,)),
            dma((PIECES, 2)),
            dma((PIECES,)),
            dma((2,)),
            dma((5,)),
            pltpu.SemaphoreType.REGULAR((1,)),
        ],
        compiler_params=pltpu.CompilerParams(
            collective_id=0, has_side_effects=True, vmem_limit_bytes=52 << 20
        ),
    )(*(in_hbm(x) for x in (signal[0], cotangent[0], record_id, rate.T, residue.T)))
    grad, terms = pl.pallas_call(
        store,
        out_shape=(
            jax.ShapeDtypeStruct((length, width), BF16),
            jax.ShapeDtypeStruct((modes, filters), F32),
        ),
        in_specs=[vmem, vmem, vmem],
        out_specs=(hbm, hbm),
        scratch_shapes=[pltpu.VMEM((modes, filters), F32), dma((2,))],
    )(in_vmem(grad), in_vmem(total), in_vmem(norm))
    return grad[None], terms.T


def solution(mesh):
    return jax.shard_map(
        body,
        mesh=mesh,
        in_specs=(P("dp", "ctx", None), P("dp", "ctx", None), P("dp", "ctx"), P(), P()),
        out_specs=(P("dp", "ctx", None), P()),
        check_vma=False,
    )
```

```python
import functools
import math

import jax
import jax.numpy as jnp
from jax import lax
from jax.experimental import pallas as pl
from jax.experimental.pallas import tpu as pltpu
from jax.sharding import PartitionSpec as P

CLUSTER = 4
PIECES = 4
BACKS = (1, 2)
ONE_ROUND = 64
MESH = pl.DeviceIdType.MESH
F32 = jnp.float32
BF16 = jnp.bfloat16


def two_parts(table):
    high = table.astype(BF16)
    return high, (table - high.astype(F32)).astype(BF16)


def dot(left, right, contract=((1,), (0,))):
    return lax.dot_general(left, right, (contract, ((), ())), preferred_element_type=F32)


def row_sums(table):
    return jnp.sum(table.T, axis=0, keepdims=True)


def round_of(shards, copies):
    return shards if shards * copies <= ONE_ROUND else CLUSTER


def kernel(
    filters,
    modes,
    shards,
    scale,
    copies,
    signal_hbm,
    cotangent_hbm,
    record_hbm,
    rate_hbm,
    residue_hbm,
    grad_ref,
    total_ref,
    norm_ref,
    signal_ref,
    cotangent_ref,
    record_ref,
    rate_ref,
    residue_ref,
    rates,
    weights,
    mask,
    edges,
    starts,
    local,
    within,
    within_out,
    within_in,
    sens_out,
    sens_in,
    ends_out,
    ends_in,
    sum_out,
    sum_in,
    adj_out,
    adj_in,
    near_out,
    near_in,
    far_out,
    far_in,
    send_sem,
    sum_send,
    sens_recv,
    ends_recv,
    within_recv,
    sum_recv,
    adj_recv,
    reduce_recv,
    fetch_sem,
    entered,
):
    length = signal_ref.shape[0]
    width = signal_ref.shape[1] // filters
    share = filters // CLUSTER
    rows = share * modes
    depth = rows // PIECES
    batch = share // PIECES
    me = lax.axis_index("ctx")
    mine = lax.rem(me, CLUSTER)
    home = me - mine
    copy_of = lax.axis_index("dp")
    planes = shards // CLUSTER
    plane = me // CLUSTER
    round_size = round_of(shards, copies)
    near_count = round_size * copies
    rounds = shards // round_size
    block = me // round_size
    in_round = lax.rem(me, round_size)
    near_mine = copy_of * round_size + in_round
    bits = round_size.bit_length() - 1
    others = [copy_of] + [lax.rem(copy_of + step, copies) for step in range(1, copies)]
    far_first = sorted(range(1, near_count), key=lambda step: -step.bit_count())
    to_sens, to_ends, to_adj, to_near, to_far, to_within = range(6)

    turns = [(1 << bit) * (1 - 2 * lax.rem(me // (1 << bit), 2)) for bit in range(bits)]

    def near_spot(step):
        flips, other = step % round_size, step // round_size
        spot = me
        for bit in range(bits):
            if flips >> bit & 1:
                spot = spot + turns[bit]
        return {"ctx": spot, "dp": others[other]}

    def far_spot(step):
        return {"ctx": lax.rem(block + step, rounds) * round_size + in_round, "dp": copy_of}

    fetches = [
        pltpu.make_async_copy(source, target, fetch_sem.at[place])
        for place, (source, target) in enumerate(
            (
                (record_hbm, record_ref),
                (rate_hbm, rate_ref),
                (residue_hbm, residue_ref),
                (cotangent_hbm, cotangent_ref),
                (signal_hbm, signal_ref),
            )
        )
    ]
    for fetch in fetches:
        fetch.start()
    barrier = pltpu.get_barrier_semaphore()
    plane_count = CLUSTER * copies
    for step in range(1, plane_count):
        spot = near_spot(step // CLUSTER * round_size + step % CLUSTER)
        pl.semaphore_signal(barrier, inc=1, device_id=spot, device_id_type=MESH)

    def tell_lower(semaphore):
        for step in range(1, planes):

            @pl.when(plane - step >= 0)
            def _(step=step):
                spot = {"ctx": me - step * CLUSTER}
                pl.semaphore_signal(semaphore, inc=1, device_id=spot, device_id_type=MESH)

    higher_parts = [(copy, part) for copy in range(copies) for part in range(CLUSTER)]
    for step in range(1, planes):

        @pl.when(plane + step < planes)
        def _(step=step):
            spots = [{"ctx": me + step * CLUSTER}]
            if rounds == 1:
                spots = [
                    {"ctx": home + step * CLUSTER + part, "dp": copy}
                    for copy, part in higher_parts
                ]
            for spot in spots:
                pl.semaphore_signal(barrier, inc=1, device_id=spot, device_id_type=MESH)


    def wait_some(semaphore, count):
        @pl.when(count > 0)
        def _():
            pl.semaphore_wait(semaphore, count)

    lane = lax.broadcasted_iota(jnp.int32, (modes, length), 1).astype(F32)
    filter_lane = lax.broadcasted_iota(jnp.int32, (modes, filters), 1)
    tag_row = lax.broadcasted_iota(jnp.int32, (8, width), 0)
    row = lax.broadcasted_iota(jnp.int32, (length, length), 0)
    column = lax.broadcasted_iota(jnp.int32, (length, length), 1)
    for fetch in fetches[:3]:
        fetch.wait()
    ids = jnp.broadcast_to(record_ref[...].astype(F32), (length, length))
    first = ids[:8, :1]
    last = ids[:8, length - 1 :]
    in_first = (ids[:1] == first[:1]).astype(F32)
    in_last = (ids[:1] == last[:1]).astype(F32)
    tag = jnp.where(tag_row == 0, first, last)

    def group(index):
        return pl.ds(pl.multiple_of(index * width, width), width)

    def table_rows(index):
        return pl.ds(pl.multiple_of(index * modes, modes), modes)

    def edge_rows(index):
        return pl.ds(pl.multiple_of(index * 2 * modes, 2 * modes), 2 * modes)

    def column_of(ref, index):
        return jnp.sum(jnp.where(filter_lane == index, ref[...], 0.0), axis=1, keepdims=True)

    def norm_of(rate):
        double = 2.0 * rate
        series = 1.0 - double * (1.0 / 6.0) * (1.0 - double * (1.0 / 7.0))
        for divisor in (5.0, 4.0, 3.0, 2.0):
            series = 1.0 - double * (1.0 / divisor) * series
        return jnp.sqrt(double * series)

    def tagged(piece):
        return pl.ds(0, depth + 8) if piece == 0 else pl.ds(8 + piece * depth, depth)

    def plain(piece):
        return pl.ds(piece * depth, depth)

    def to_peer(source, target, send, recv, step):
        return pltpu.make_async_remote_copy(
            src_ref=source,
            dst_ref=target,
            send_sem=send_sem.at[send],
            recv_sem=recv,
            device_id={"ctx": home + lax.rem(mine + step, CLUSTER)},
            device_id_type=MESH,
        )

    def sens_copy(piece, step):
        peer = lax.rem(mine + step, CLUSTER)
        return to_peer(
            sens_out.at[peer, tagged(piece)],
            sens_in.at[mine, tagged(piece)],
            to_sens,
            sens_recv.at[piece],
            step,
        )

    def adj_copy(piece, step):
        peer = lax.rem(mine + step, CLUSTER)
        return to_peer(
            adj_out.at[peer, plain(piece)],
            adj_in.at[mine, plain(piece)],
            to_adj,
            adj_recv.at[piece],
            step,
        )

    def wait_peers(ref, span, send, recv):
        several = ref.at[pl.ds(0, CLUSTER - 1), span]
        to_peer(several, several, send, recv, 1).wait_recv()

    def wait_sent(ref, send):
        several = ref.at[pl.ds(0, CLUSTER - 1)]
        to_peer(several, several, send, ends_recv.at[0], 1).wait_send()

    def sum_copy(piece, back):
        return pltpu.make_async_remote_copy(
            src_ref=sum_out.at[tagged(piece)],
            dst_ref=sum_in.at[back - 1, tagged(piece)],
            send_sem=sum_send.at[back - 1],
            recv_sem=sum_recv.at[piece, back - 1],
            device_id={"ctx": me - back * CLUSTER},
            device_id_type=MESH,
        )

    def prepare(index):
        rate = jnp.broadcast_to(column_of(rate_ref, index), (modes, width))
        rates[table_rows(index), :] = rate
        high, low = two_parts(jnp.exp(-rate * (lane + 1.0)) * in_first)
        starts[edge_rows(index), :] = jnp.concatenate([high, low], axis=0)

    def sense(index):
        both = dot(starts[edge_rows(index), :], cotangent_ref[:, group(index)])
        spot = pl.ds(pl.multiple_of(8 + lax.rem(index, share) * modes, 8), modes)
        sens_out[index // share, spot, :] = both[:modes] + both[modes:]

    def weigh(index, carry):
        norm = norm_of(rates[table_rows(index), :])
        weights[table_rows(index), :] = norm * column_of(residue_ref, index)
        return carry

    def end(index):
        rate = rates[table_rows(index), :]
        high, low = two_parts(jnp.exp(-rate * (length - 1.0 - lane)) * in_last)
        pair = jnp.concatenate([high, low], axis=0)
        edges[edge_rows(index), :] = pair
        both = dot(pair, signal_ref[:, group(index)])
        spot = pl.ds(pl.multiple_of(lax.rem(index, share) * modes, modes), modes)
        ends_out[index // share, spot, :] = both[:modes] + both[modes:]

    row_of = lax.broadcasted_iota(jnp.int32, (8, length), 0)

    def intra(index, carry):
        rate = rates[table_rows(index), :]
        products = dot(signal_ref[:, group(index)], cotangent_ref[:, group(index)], ((1,), (1,)))
        products = products * mask[...]
        parts = [products[:8]]
        for start in range(8, length, 8):
            parts.append(pltpu.roll(products[start : start + 8], length - start, 1))
        while len(parts) > 1:
            parts = [parts[i] + parts[i + 1] for i in range(0, len(parts), 2)]
        by_lag = parts[0]
        for bit in (1, 2, 4):
            moved = pltpu.roll(by_lag, length - bit, 1)
            by_lag = jnp.where((row_of & bit) != 0, moved, by_lag)
        by_lag = jnp.sum(by_lag, axis=0, keepdims=True)
        within[table_rows(index), :] = by_lag * jnp.exp(-rate * lane)
        return carry

    def near_by(index, carry):
        rate = rates[table_rows(index), :]
        weight = weights[table_rows(index), :]
        lags = jnp.sum(weight * jnp.exp(-rate * lane), axis=0, keepdims=True)
        spread = pltpu.roll(
            jnp.broadcast_to(lags, (length, length)), 0, 1, stride=1, stride_axis=0
        )
        kernel_now = (spread * mask[...]).astype(BF16)
        local[:, group(index)] = dot(kernel_now, cotangent_ref[:, group(index)])
        return carry

    for part in range(CLUSTER):
        sens_out[part, :8, :] = tag
    for back in BACKS:

        @pl.when(me + back * CLUSTER >= shards)
        def _(back=back):
            sum_in[back - 1] = jnp.full(sum_in.shape[1:], -1.0, F32)

    for index in range(filters):
        prepare(index)
    fetches[3].wait()
    for piece in range(PIECES):
        for step in (2, 1, 3, 0):
            base = lax.rem(mine + step, CLUSTER) * share + piece * batch
            for index in range(batch):
                sense(base + index)
        if piece == 0:
            pl.semaphore_wait(barrier, plane_count - 1 + plane * (plane_count if rounds == 1 else 1))
            tell_lower(entered.at[0])
        for step in (3, 1, 2):
            sens_copy(piece, step).start()
        sens_in[mine, tagged(piece), :] = sens_out[mine, tagged(piece), :]
    mask[...] = jnp.where((ids == ids.T) & (column >= row), 1.0, 0.0)
    fetches[4].wait()
    for piece in range(PIECES):
        for step in (2, 1, 3, 0):
            base = lax.rem(mine + step, CLUSTER) * share + piece * batch
            for index in range(batch):
                end(base + index)
    for step in (3, 1, 2):
        peer = lax.rem(mine + step, CLUSTER)
        to_peer(ends_out.at[peer], ends_in.at[mine], to_ends, ends_recv.at[0], step).start()
    for piece in range(PIECES):
        ends_in[mine, plain(piece), :] = ends_out[mine, plain(piece), :]

    def decay_of(piece):
        start = pl.multiple_of(mine * rows + piece * depth, 8)
        return jnp.exp(-rates[pl.ds(start, depth), :] * float(length))


    for piece in range(PIECES):
        if piece == 1:
            lax.fori_loop(0, filters, intra, 0, unroll=16)
            for part in range(CLUSTER):
                within_out[part] = row_sums(within[part * rows : (part + 1) * rows, :])
            for step in (3, 1, 2):
                peer = lax.rem(mine + step, CLUSTER)
                to_peer(
                    within_out.at[peer], within_in.at[mine], to_within, within_recv.at[0], step
                ).start()
            within_in[mine] = within_out[mine]
        wait_peers(sens_in, tagged(piece), to_sens, sens_recv.at[piece])
        decay = decay_of(piece)
        firsts = [sens_in[place, 0:1, :] for place in range(CLUSTER)]
        lasts = [sens_in[place, 1:2, :] for place in range(CLUSTER)]
        span = pl.ds(8 + piece * depth, depth)
        values = []
        value = jnp.zeros((depth, width), F32)
        for place in range(CLUSTER - 1, -1, -1):
            values.append(value)
            value = jnp.where(firsts[place] == lasts[place], decay * value, 0.0)
            value = sens_in[place, span, :] + value
            if place:
                value = jnp.where(firsts[place] == lasts[place - 1], value, 0.0)
        sum_out[span, :] = value
        if piece == 0:
            sum_out[:8, :] = sens_in[0, :8, :]
        for back in BACKS:

            @pl.when(me - back * CLUSTER >= 0)
            def _(piece=piece, back=back):
                sum_copy(piece, back).start()

        for place, value in enumerate(reversed(values)):
            adj_out[place, plain(piece), :] = value


    for piece in range(PIECES):
        for back in BACKS:

            @pl.when(me + back * CLUSTER < shards)
            def _(piece=piece, back=back):
                sum_copy(piece, back).wait_recv()

        decay = decay_of(piece)
        span = pl.ds(8 + piece * depth, depth)
        fourth = decay * decay
        fourth = fourth * fourth
        moved = [sum_in[0, span, :], fourth * sum_in[1, span, :]]
        for place in range(CLUSTER - 1, -1, -1):
            value = adj_out[place, plain(piece), :]
            for back in BACKS:
                hit = sum_in[back - 1, 0:1, :] == sens_in[place, 1:2, :]
                value = value + jnp.where(hit, moved[back - 1], 0.0)
            adj_out[place, plain(piece), :] = value
            if place:
                moved = [decay * value for value in moved]
        for step in (3, 1, 2):
            adj_copy(piece, step).start()
        adj_in[mine, plain(piece), :] = adj_out[mine, plain(piece), :]

    wait_some(entered.at[0], planes - 1 - plane)
    wait_peers(ends_in, pl.ds(0, rows), to_ends, ends_recv.at[0])
    product = ends_in[0] * adj_out[0]
    for place in range(1, CLUSTER):
        product = product + ends_in[place] * adj_out[place]
    wait_peers(within_in, pl.ds(0, 1), to_within, within_recv.at[0])
    terms = row_sums(product)
    for place in range(CLUSTER):
        terms = terms + within_in[place]
    near_out[0] = terms

    def near_copy(step):
        return pltpu.make_async_remote_copy(
            src_ref=near_out.at[0],
            dst_ref=near_in.at[near_mine],
            send_sem=send_sem.at[to_near],
            recv_sem=reduce_recv.at[0],
            device_id=near_spot(step),
            device_id_type=MESH,
        )

    def far_copy(step):
        return pltpu.make_async_remote_copy(
            src_ref=far_out,
            dst_ref=far_in.at[block],
            send_sem=send_sem.at[to_far],
            recv_sem=reduce_recv.at[1],
            device_id=far_spot(step),
            device_id_type=MESH,
        )

    def all_of(ref, count, send, recv):
        several = ref.at[pl.ds(0, count)]
        return to_peer(several, several, send, recv, 1)

    near_all = all_of(near_in, near_count - 1, to_near, reduce_recv.at[0])
    far_all = all_of(far_in, rounds - 1, to_far, reduce_recv.at[1]) if rounds > 1 else None

    for step in far_first:
        near_copy(step).start()
    near_in[near_mine] = near_out[0]
    norm_ref[...] = norm_of(rate_ref[...]) * scale

    lax.fori_loop(0, filters, weigh, 0, unroll=16)
    lax.fori_loop(0, filters, near_by, 0, unroll=16)

    def gather_near():
        near_all.wait_recv()
        for part in range(CLUSTER):
            total = near_in[part]
            for rank in range(part + CLUSTER, near_count, CLUSTER):
                total = total + near_in[rank]
            total_ref[part : part + 1, :] = total

    if rounds > 1:
        gather_near()
        far_out[...] = total_ref[...]
        for step in range(1, rounds):
            far_copy(step).start()
        far_in[block] = far_out[...]

    def finish(index):
        high_low = edges[edge_rows(index), :]
        spot = pl.ds(pl.multiple_of(lax.rem(index, share) * modes, modes), modes)
        adjoint = adj_in[index // share, spot, :]
        adj_high, adj_low = two_parts(weights[table_rows(index), :] * adjoint)
        left = jnp.concatenate([high_low, high_low[:modes]], axis=0)
        right = jnp.concatenate([adj_high, adj_high, adj_low], axis=0)
        carried = dot(left, right, ((0,), (0,)))
        grad_ref[:, group(index)] = (local[:, group(index)] + carried).astype(BF16)

    for piece in range(PIECES):
        wait_peers(adj_in, plain(piece), to_adj, adj_recv.at[piece])

        def finish_one(turn, carry, piece=piece):
            finish(turn // batch * share + piece * batch + lax.rem(turn, batch))
            return carry

        lax.fori_loop(0, CLUSTER * batch, finish_one, 0, unroll=8)

    if rounds > 1:
        far_all.wait_recv()
        far_total = far_in[0]
        for rank in range(1, rounds):
            far_total = far_total + far_in[rank]
        total_ref[...] = far_total
    else:
        gather_near()

    wait_sent(sens_out, to_sens)
    wait_sent(ends_out, to_ends)
    wait_sent(adj_out, to_adj)
    wait_sent(within_out, to_within)
    near_all.wait_send()
    if rounds > 1:
        far_all.wait_send()
    for back in BACKS:

        @pl.when(me - back * CLUSTER >= 0)
        def _(back=back):
            pltpu.make_async_remote_copy(
                src_ref=sum_out,
                dst_ref=sum_in.at[back - 1],
                send_sem=sum_send.at[back - 1],
                recv_sem=sum_recv.at[0, back - 1],
                device_id={"ctx": me - back * CLUSTER},
                device_id_type=MESH,
            ).wait_send()


def store(grad_ref, total_ref, norm_ref, grad_hbm, term_hbm, term_ref, sems):
    write_grad = pltpu.make_async_copy(grad_ref, grad_hbm, sems.at[0])
    write_grad.start()
    modes, filters = norm_ref.shape
    parts, rows = total_ref.shape
    share = filters // parts
    row = lax.broadcasted_iota(jnp.int32, (rows, filters), 0)
    column = lax.broadcasted_iota(jnp.int32, (rows, filters), 1)
    lane = lax.broadcasted_iota(jnp.int32, (modes, rows), 1)
    mode = lax.broadcasted_iota(jnp.int32, (modes, rows), 0)
    own = (lane & (modes - 1)) == mode
    total = jnp.zeros((3 * modes, filters), F32)
    for part in range(parts):
        spread = jnp.where(own, total_ref[part : part + 1, :], 0.0)
        high, rest = spread.astype(BF16), spread - spread.astype(BF16).astype(F32)
        middle, low = two_parts(rest)
        start = (column - part * share) * modes
        pick = jnp.where((row >= start) & (row < start + modes), 1.0, 0.0).astype(BF16)
        total = total + dot(jnp.concatenate([high, middle, low], axis=0), pick)
    total = total[:modes] + (total[modes : 2 * modes] + total[2 * modes :])
    term_ref[...] = norm_ref[...] * total
    write_term = pltpu.make_async_copy(term_ref, term_hbm, sems.at[1])
    write_term.start()
    write_term.wait()
    write_grad.wait()


def body(signal, cotangent, record_id, rate, residue):
    length, width = signal.shape[1:]
    filters, modes = rate.shape
    shards = lax.axis_size("ctx")
    group_width = width // filters
    rows = filters // CLUSTER * modes
    sequences = signal.shape[0] * lax.axis_size("dp")
    scale = 1.0 / math.sqrt(sequences * length * shards * group_width)
    copies = lax.axis_size("dp")
    near_count = round_of(shards, copies) * copies
    rounds = shards // round_of(shards, copies)
    hbm = pl.BlockSpec(memory_space=pltpu.HBM)
    vmem = pl.BlockSpec(memory_space=pltpu.VMEM)
    in_hbm = functools.partial(pltpu.with_memory_space_constraint, memory_space=pltpu.HBM)
    in_vmem = functools.partial(pltpu.with_memory_space_constraint, memory_space=pltpu.VMEM)
    dma = pltpu.SemaphoreType.DMA
    grad, total, norm = pl.pallas_call(
        functools.partial(kernel, filters, modes, shards, scale, copies),
        out_shape=(
            pltpu.VMEM((length, width), BF16),
            pltpu.VMEM((CLUSTER, rows), F32),
            pltpu.VMEM((modes, filters), F32),
        ),
        in_specs=[hbm] * 5,
        out_specs=(vmem, vmem, vmem),
        scratch_shapes=[
            pltpu.VMEM((length, width), BF16),
            pltpu.VMEM((length, width), BF16),
            pltpu.VMEM(record_id.shape, jnp.int32),
            pltpu.VMEM((modes, filters), F32),
            pltpu.VMEM((modes, filters), F32),
            pltpu.VMEM((filters * modes, group_width), F32),
            pltpu.VMEM((filters * modes, group_width), F32),
            pltpu.VMEM((length, length), F32),
            pltpu.VMEM((filters * 2 * modes, length), BF16),
            pltpu.VMEM((filters * 2 * modes, length), BF16),
            pltpu.VMEM((length, width), F32),
            pltpu.VMEM((filters * modes, length), F32),
            pltpu.VMEM((CLUSTER, 1, rows), F32),
            pltpu.VMEM((CLUSTER, 1, rows), F32),
            pltpu.VMEM((CLUSTER, rows + 8, group_width), F32),
            pltpu.VMEM((CLUSTER, rows + 8, group_width), F32),
            pltpu.VMEM((CLUSTER, rows, group_width), F32),
            pltpu.VMEM((CLUSTER, rows, group_width), F32),
            pltpu.VMEM((rows + 8, group_width), F32),
            pltpu.VMEM((2, rows + 8, group_width), F32),
            pltpu.VMEM((CLUSTER, rows, group_width), F32),
            pltpu.VMEM((CLUSTER, rows, group_width), F32),
            pltpu.VMEM((1, 1, rows), F32),
            pltpu.VMEM((near_count, 1, rows), F32),
            pltpu.VMEM((CLUSTER, rows), F32),
            pltpu.VMEM((rounds, CLUSTER, rows), F32),
            dma((6,)),
            dma((2,)),
            dma((PIECES,)),
            dma((1,)),
            dma((1,)),
            dma((PIECES, 2)),
            dma((PIECES,)),
            dma((2,)),
            dma((5,)),
            pltpu.SemaphoreType.REGULAR((1,)),
        ],
        compiler_params=pltpu.CompilerParams(
            collective_id=0, has_side_effects=True, vmem_limit_bytes=52 << 20
        ),
    )(*(in_hbm(x) for x in (signal[0], cotangent[0], record_id, rate.T, residue.T)))
    grad, terms = pl.pallas_call(
        store,
        out_shape=(
            jax.ShapeDtypeStruct((length, width), BF16),
            jax.ShapeDtypeStruct((modes, filters), F32),
        ),
        in_specs=[vmem, vmem, vmem],
        out_specs=(hbm, hbm),
        scratch_shapes=[pltpu.VMEM((modes, filters), F32), dma((2,))],
    )(in_vmem(grad), in_vmem(total), in_vmem(norm))
    return grad[None], terms.T


def solution(mesh):
    return jax.shard_map(
        body,
        mesh=mesh,
        in_specs=(P("dp", "ctx", None), P("dp", "ctx", None), P("dp", "ctx"), P(), P()),
        out_specs=(P("dp", "ctx", None), P()),
        check_vma=False,
    )
```
